32 devices in a mesh: row: 4 (over x, core), col: 8 (over z, y).
Axes of the slice: x: 2, y: 2, z: 4, core: 2. Of those that a mesh axis runs over, the one named last changes fastest.
Arguments:
- masters: float32 [128, 4096], P('col'), may hold values from -6 to 6
- inst_master: int32 [64, 128], P('row', 'col'), may hold values from 0 to 127
- inst_orient: int32 [64, 128], P('row', 'col'), may hold values from 0 to 3
- owner_map: int32 [128], replicated, may hold values from 0 to 127, each once
- tile_free: float32 [4096, 8192], P('row', 'col'), may hold values from -3 to 3
- target: float32 [4096, 8192], P('row', 'col'), may hold values from 0 to 1
- kernel_spectra: float32 [2, 128, 8, 128], replicated, may hold values from -6 to 6
- socs_weights: float32 [8], replicated, may hold values from 0.05 to 1
Outputs:
- resist: float32 [4096, 8192], P('row', 'col')
- new_mask: float32 [4096, 8192], P('row', 'col')
- masters_out: float32 [128, 4096], P('col')
The draws below stay inside these ranges and needn't reach their ends.
Inputs may be any that keep to these rules, and one draw needn't show every extreme that they name: `inst_orient`: bit 0 reverses a cell's rows, bit 1 its columns. `owner_map`: each storage row is used by exactly one master; storage row r lies on index r // 16 of col.
All inputs are finite; a program needn't handle non-finite values.
Results may differ from the reference program's by a relative error of at most 0.0092.
Values may be sent and summed in bfloat16 or wider, within the bound.
A program may use at most 128 MiB of HBM per device.

```python
import math
import jax
import jax.numpy as jnp
import numpy as np
from jax import lax

TILE = 512
TPD = 2
HALO = 64
CELL = 64
BAND = 128
NK = 8
ITERS = 1
PAD = 640
NM = 128
ROWS = 4096
COLS = 8192
GRID_R = 64
GRID_C = 128
N_ROW = 4
N_COL = 8


def place_ends(values, own_key, least, high):
    dims = values.shape
    spot = [jax.random.randint(jax.random.fold_in(own_key, axis), (), 0, dims[axis]) for axis in range(len(dims))]
    values = values.at[tuple(spot)].set(least)
    longest = dims.index(max(dims))
    spot[longest] = (spot[longest] + 1) % dims[longest]
    return values.at[tuple(spot)].set(high)


def block_scale(rng, extent, shards, low, largest):
    def one(position, shards_of):
        draws = jax.random.uniform(jax.random.fold_in(jax.random.fold_in(rng, 6), position), (shards_of,), jnp.float32, low / len(shards), largest / len(shards))
        return jnp.repeat(jnp.exp(draws), extent[position] // shards_of).reshape((-1,) + (1,) * (len(extent) - position - 1))

    gain = one(*shards[0])
    for cut in shards[1:]:
        gain = gain * one(*cut)
    return gain


def rank_bounds(count, skew):
    portions = [(1 << 20) // math.isqrt(standing ** skew) + 1 for standing in range(1, count + 1)]
    deviation = 1 + sum(portions) // (1 << 30)
    return np.cumsum(np.array([max(1, weight // deviation) for weight in portions]))


def ranked(own_key, shape, count, slope):
    listing = rank_bounds(count, slope)
    lot = jax.random.randint(jax.random.fold_in(own_key, 1), shape, 0, int(listing[count - 1]))
    standing = jnp.searchsorted(jnp.asarray(listing, jnp.int32), lot, side="right")
    return jax.random.permutation(jax.random.fold_in(own_key, 2), count)[standing].astype(jnp.int32)


def bell_draw(stream_key, extent, deviation, reach, shards=(), kind=jnp.bfloat16):
    gain = block_scale(stream_key, extent, shards, -0.22, 0.18) if shards else 1.0
    entries = jax.random.normal(stream_key, extent, jnp.float32) * deviation * gain
    return jnp.minimum(jnp.maximum(entries, -reach), reach).astype(kind)


def setup_inputs(seed: int = 0) -> dict:
    key_of = jax.random.split(jax.random.key(seed), 9)
    return {
        "masters": bell_draw(key_of[0], (NM, CELL * CELL), 1.0, 6.0, ((0, 8),), jnp.float32),
        "inst_master": place_ends(ranked(key_of[1], (GRID_R, GRID_C), NM, 2), jax.random.fold_in(key_of[1], 3), 0, NM - 1).astype(jnp.int32),
        "inst_orient": place_ends(jax.random.randint(key_of[2], (GRID_R, GRID_C), 0, 4), jax.random.fold_in(key_of[2], 1), 0, 3).astype(jnp.int32),
        "owner_map": jax.random.permutation(key_of[3], NM).astype(jnp.int32),
        "tile_free": bell_draw(key_of[4], (ROWS, COLS), 0.5, 3.0, ((0, 4), (1, 8)), jnp.float32),
        "target": jnp.clip(1.0 * jax.random.uniform(key_of[5], (ROWS, COLS), jnp.float32) ** block_scale(key_of[5], (ROWS, COLS), ((0, 4), (1, 8)), -0.2, 0.2), 0.0, 1.0),
        "kernel_spectra": bell_draw(key_of[6], (2, BAND, NK, BAND), 1.0, 6.0, (), jnp.float32),
        "socs_weights": jnp.clip(jnp.exp(jax.random.uniform(key_of[7], (NK,), jnp.float32, math.log(0.05), math.log(1.0))), 0.05, 1.0),
    }


step_free = 1.0
step_master = 0.05
resist_gain = 2.0
resist_level = 1.8


def dot_plain(left, right):
    return jnp.dot(left, right, preferred_element_type=jnp.float32)


def dot_right_t(left, right):
    return lax.dot_general(left, right, (((1,), (1,)), ((), ())), preferred_element_type=jnp.float32)


def dot_left_t(left, right):
    return lax.dot_general(left, right, (((0,), (0,)), ((), ())), preferred_element_type=jnp.float32)


def tables(pad_side, band_side):
    freqs = jnp.arange(band_side, dtype=jnp.int32) - band_side // 2
    pixels = jnp.arange(pad_side, dtype=jnp.int32)
    phases = (freqs[:, None] * pixels[None, :]) % pad_side
    angles = phases.astype(jnp.float32) * (2.0 * math.pi / pad_side)
    return jnp.cos(angles).astype(jnp.bfloat16), jnp.sin(angles).astype(jnp.bfloat16)


def tile_step(padded, target, spectra, weights, halo_side):
    pad_side = padded.shape[0]
    band_side = spectra.shape[1]
    kernels = spectra.shape[2]
    tile_side = pad_side - 2 * halo_side
    cos_full, sin_full = tables(pad_side, band_side)
    cos_in = cos_full[:, halo_side:halo_side + tile_side]
    sin_in = sin_full[:, halo_side:halo_side + tile_side]
    forw_re = dot_plain(cos_full, padded).astype(jnp.bfloat16)
    forw_im = (-dot_plain(sin_full, padded)).astype(jnp.bfloat16)
    spec_re = (dot_right_t(forw_re, cos_full) - dot_right_t(forw_im, sin_full)) / pad_side
    spec_im = (-dot_right_t(forw_re, sin_full) - dot_right_t(forw_im, cos_full)) / pad_side
    kern_re = spectra[0]
    kern_im = spectra[1]
    amp_re = (kern_re * spec_re[:, None, :] - kern_im * spec_im[:, None, :]).astype(jnp.bfloat16)
    amp_im = (kern_re * spec_im[:, None, :] + kern_im * spec_re[:, None, :]).astype(jnp.bfloat16)
    amp_re = amp_re.reshape(band_side, kernels * band_side)
    amp_im = amp_im.reshape(band_side, kernels * band_side)
    half_re = (dot_left_t(cos_in, amp_re) - dot_left_t(sin_in, amp_im)).astype(jnp.bfloat16)
    half_im = (dot_left_t(cos_in, amp_im) + dot_left_t(sin_in, amp_re)).astype(jnp.bfloat16)
    half_re = half_re.reshape(tile_side * kernels, band_side)
    half_im = half_im.reshape(tile_side * kernels, band_side)
    field_re = (dot_plain(half_re, cos_in) - dot_plain(half_im, sin_in)) / band_side
    field_im = (dot_plain(half_re, sin_in) + dot_plain(half_im, cos_in)) / band_side
    field_re = field_re.reshape(tile_side, kernels, tile_side)
    field_im = field_im.reshape(tile_side, kernels, tile_side)
    scaled = weights[None, :, None]
    intensity = jnp.sum(scaled * (field_re * field_re + field_im * field_im), axis=1)
    resist = jax.nn.sigmoid(resist_gain * (intensity - resist_level))
    slopes = 2.0 * (resist - target) * resist_gain * resist * (1.0 - resist)
    back_re = (2.0 / band_side * scaled * slopes[:, None, :] * field_re).astype(jnp.bfloat16)
    back_im = (2.0 / band_side * scaled * slopes[:, None, :] * field_im).astype(jnp.bfloat16)
    back_re = back_re.reshape(tile_side * kernels, tile_side)
    back_im = back_im.reshape(tile_side * kernels, tile_side)
    bhalf_re = (dot_right_t(back_re, cos_in) + dot_right_t(back_im, sin_in)).astype(jnp.bfloat16)
    bhalf_im = (dot_right_t(back_im, cos_in) - dot_right_t(back_re, sin_in)).astype(jnp.bfloat16)
    bhalf_re = bhalf_re.reshape(tile_side, kernels * band_side)
    bhalf_im = bhalf_im.reshape(tile_side, kernels * band_side)
    bamp_re = (dot_plain(cos_in, bhalf_re) + dot_plain(sin_in, bhalf_im)).reshape(band_side, kernels, band_side)
    bamp_im = (dot_plain(cos_in, bhalf_im) - dot_plain(sin_in, bhalf_re)).reshape(band_side, kernels, band_side)
    bspec_re = (jnp.sum(kern_re * bamp_re + kern_im * bamp_im, axis=1) / pad_side).astype(jnp.bfloat16)
    bspec_im = (jnp.sum(kern_re * bamp_im - kern_im * bamp_re, axis=1) / pad_side).astype(jnp.bfloat16)
    bforw_re = (dot_plain(bspec_re, cos_in) - dot_plain(bspec_im, sin_in)).astype(jnp.bfloat16)
    bforw_im = (-dot_plain(bspec_re, sin_in) - dot_plain(bspec_im, cos_in)).astype(jnp.bfloat16)
    gradient = dot_left_t(cos_in, bforw_re) - dot_left_t(sin_in, bforw_im)
    return resist, gradient


def orient_cells(cells, orient):
    flip_first = (orient % 2) == 1
    flip_second = (orient // 2) == 1
    cells = jnp.where(flip_first[..., None, None], cells[..., ::-1, :], cells)
    cells = jnp.where(flip_second[..., None, None], cells[..., :, ::-1], cells)
    return cells


def assemble(master_rows, slots, orient, cell_side):
    grid_rows, grid_cols = slots.shape
    cells = jnp.take(master_rows, slots.reshape(-1), axis=0)
    cells = cells.reshape(grid_rows, grid_cols, cell_side, cell_side)
    cells = orient_cells(cells, orient)
    return cells.transpose(0, 2, 1, 3).reshape(grid_rows * cell_side, grid_cols * cell_side)


def cells_of(image, orient, cell_side):
    grid_rows, grid_cols = orient.shape
    cells = image.reshape(grid_rows, cell_side, grid_cols, cell_side).transpose(0, 2, 1, 3)
    cells = orient_cells(cells, orient)
    return cells.reshape(grid_rows * grid_cols, cell_side * cell_side)


def smooth(master_rows, cell_side):
    grids = master_rows.reshape(-1, cell_side, cell_side)
    framed = jnp.pad(grids, ((0, 0), (1, 1), (1, 1)))
    beside_all = framed[:, 2:, 1:-1] + framed[:, :-2, 1:-1] + framed[:, 1:-1, 2:] + framed[:, 1:-1, :-2]
    return (0.5 * grids + 0.125 * beside_all).reshape(master_rows.shape)


def stitch(tiles, tile_rows, tile_cols):
    return tiles.reshape(tile_rows, tile_cols, TILE, TILE).transpose(0, 2, 1, 3).reshape(tile_rows * TILE, tile_cols * TILE)


def reference(masters, inst_master, inst_orient, owner_map, tile_free, target, kernel_spectra, socs_weights):
    slots = jnp.take(owner_map, inst_master)
    master_rows = masters
    free_field = tile_free
    resist = jnp.zeros_like(tile_free)
    tile_rows = N_ROW * TPD
    tile_cols = N_COL * TPD
    for sweep_index in range(ITERS):
        shading = jnp.tanh(assemble(master_rows, slots, inst_orient, CELL) + free_field)
        framed = jnp.pad(shading.astype(jnp.bfloat16), HALO)

        def one_tile(tile_index):
            row_at = tile_index // tile_cols
            col_at = tile_index % tile_cols
            window = lax.dynamic_slice(framed, (row_at * TILE, col_at * TILE), (PAD, PAD))
            goal_tile = lax.dynamic_slice(target, (row_at * TILE, col_at * TILE), (TILE, TILE))
            return tile_step(window, goal_tile, kernel_spectra, socs_weights, HALO)

        resist_tiles, grad_tiles = lax.map(one_tile, jnp.arange(tile_rows * tile_cols, dtype=jnp.int32))
        resist = stitch(resist_tiles, tile_rows, tile_cols)
        grad_param = stitch(grad_tiles, tile_rows, tile_cols) * (1.0 - shading * shading)
        free_field = free_field - step_free * grad_param
        cell_grads = cells_of(grad_param, inst_orient, CELL)
        master_grad = jax.ops.segment_sum(cell_grads, slots.reshape(-1), num_segments=NM)
        master_rows = smooth(master_rows - step_master * master_grad, CELL)
    new_mask = jnp.tanh(assemble(master_rows, slots, inst_orient, CELL) + free_field)
    return resist, new_mask, master_rows
```

```python
import functools
import math

import jax
import jax.numpy as jnp
import numpy as np
from jax import lax
from jax.experimental import pallas as pl
from jax.experimental.pallas import tpu as pltpu
from jax.sharding import PartitionSpec as P

TILE = 512
TPD = 2
HALO = 64
CELL = 64
LANES = 128
HALF = CELL // 2
STRIP = 16
GROUP = 4

step_free = 1.0
step_master = 0.05
resist_gain = 2.0
resist_level = 1.8


def dot(left, right):
    return jnp.dot(left, right, preferred_element_type=jnp.float32)


def bfloat(value):
    return jnp.asarray(np.ascontiguousarray(value).astype(jnp.bfloat16))


def tables(pad_side, band_side, halo, tile):
    freqs = np.arange(band_side, dtype=np.int64) - band_side // 2
    phases = (freqs[:, None] * np.arange(pad_side)[None, :]) % pad_side
    angles = phases.astype(np.float32) * np.float32(2.0 * math.pi / pad_side)
    cos = np.cos(angles)
    sin = np.sin(angles)
    cos_in = cos[:, halo : halo + tile]
    sin_in = sin[:, halo : halo + tile]
    cs_full = np.concatenate([cos, sin], 0)
    cs_lanes = np.pad(cs_full, ((0, 0), (LANES - halo, LANES - halo)))
    cs_in = np.concatenate([cos_in, sin_in], 0)
    grid = 2 * band_side
    turns = (freqs[:, None] * np.arange(grid)[None, :]) % grid
    cos_g = np.cos(turns * (2.0 * math.pi / grid))
    sin_g = np.sin(turns * (2.0 * math.pi / grid))
    cs_g = np.concatenate([cos_g, sin_g], 0)
    field = np.block([[cos_g, sin_g], [-sin_g, cos_g]])
    gaps = np.arange(halo, halo + tile)[:, None] / pad_side - np.arange(grid)[None, :] / grid
    waves = np.arange(1, band_side)
    spread = (1.0 + 2.0 * np.cos(2.0 * math.pi * gaps[:, :, None] * waves).sum(-1)) / grid
    parts = (cs_full, cs_lanes.T, cs_g, cs_g.T, field, field.T, spread, spread.T, cs_in, cs_in.T)
    return [bfloat(p) for p in parts]


def flips():
    back = np.eye(CELL)[::-1]
    rows = np.kron(np.eye(4), back)
    same = np.eye(CELL)
    none = np.zeros((CELL, CELL))
    spread = [
        np.block([[m, m], [none, none]]) if e == 0 else np.block([[none, none], [m, m]])
        for m in (same, back)
        for e in range(2)
    ]
    return bfloat(rows), bfloat(np.concatenate(spread, 1))


def left_mask(rows):
    return lax.broadcasted_iota(jnp.int32, (rows, LANES), 1) < CELL


def pair_codes(inst_ref, orient_ref, owner_ref, a, b):
    s0 = owner_ref[inst_ref[a, b]]
    s1 = owner_ref[inst_ref[a, b + 1]]
    return s0, s1, orient_ref[a, b], orient_ref[a, b + 1]


def build_turned(table_ref, turned_ref, flip_ref, spread_ref):
    def step(b, carry):
        at = pl.ds(b * 4, 4)
        cells = table_ref[at].reshape(4 * CELL, LANES)
        flipped = dot(flip_ref[...], cells).astype(jnp.bfloat16)
        for f, part in enumerate((cells, flipped)):
            both = dot(part, spread_ref[...]).astype(jnp.bfloat16)
            for c in range(2):
                for e in range(2):
                    lanes = slice((2 * c + e) * LANES, (2 * c + e + 1) * LANES)
                    turned_ref[2 * c + f, at, e] = both[:, lanes].reshape(4, CELL, LANES)
        return carry

    lax.fori_loop(0, table_ref.shape[0] // 4, step, 0)


def assemble_pair(turned_ref, codes):
    s0, s1, o0, o1 = codes
    one = turned_ref[o0, s0 // 2, s0 % 2].astype(jnp.float32)
    two = turned_ref[o1, s1 // 2, s1 % 2].astype(jnp.float32)
    return jnp.where(left_mask(CELL), one, two)


def image_kernel(
    emit_mask, inst_ref, orient_ref, owner_ref, table_ref, free_ref, flip_ref, spread_ref, *rest
):
    *outs, turned_s = rest
    a = pl.program_id(0)

    @pl.when(a == 0)
    def _():
        build_turned(table_ref, turned_s, flip_ref, spread_ref)

    pairs = free_ref.shape[1] // LANES
    for pair in range(pairs):
        codes = pair_codes(inst_ref, orient_ref, owner_ref, a, 2 * pair)
        cells = assemble_pair(turned_s, codes)
        lanes = slice(pair * LANES, (pair + 1) * LANES)
        value = jnp.tanh(cells + free_ref[:, lanes])
        outs[0][:, lanes] = value.astype(outs[0].dtype)
        if emit_mask:
            left = left_mask(HALF)
            if pair == 0:
                turned = pltpu.roll(value[HALF:], CELL, 1)
                outs[1][...] = jnp.where(left, value[:HALF], turned).astype(jnp.bfloat16)
            if pair == pairs - 1:
                turned = pltpu.roll(value[:HALF], CELL, 1)
                outs[2][...] = jnp.where(left, turned, value[HALF:]).astype(jnp.bfloat16)


def whole_spec(array):
    zeros = (0,) * array.ndim
    return pl.BlockSpec(array.shape, lambda *_: zeros)


def image(inst, orient, owner, table, free, flip, spread, emit_mask):
    height, width = free.shape
    strip = pl.BlockSpec((CELL, width), lambda a, *_: (a, 0))
    out_shape = [jax.ShapeDtypeStruct(free.shape, jnp.bfloat16 if emit_mask else jnp.float32)]
    out_specs = [strip]
    if emit_mask:
        edge = jax.ShapeDtypeStruct((height // 2, LANES), jnp.bfloat16)
        edge_spec = pl.BlockSpec((HALF, LANES), lambda a, *_: (a, 0))
        out_shape += [edge, edge]
        out_specs += [edge_spec, edge_spec]
    return pl.pallas_call(
        functools.partial(image_kernel, emit_mask),
        grid_spec=pltpu.PrefetchScalarGridSpec(
            num_scalar_prefetch=3,
            grid=(height // CELL,),
            in_specs=[whole_spec(table), strip, whole_spec(flip), whole_spec(spread)],
            out_specs=out_specs,
            scratch_shapes=[pltpu.VMEM((4, table.shape[0], 2, CELL, LANES), jnp.bfloat16)],
        ),
        out_shape=out_shape,
        name="image",
    )(inst, orient, owner, table, free, flip, spread)


def tile_kernel(
    inst_ref, orient_ref, owner_ref, weights_ref,
    padded_ref, target_ref, free_ref, spectra_ref,
    cs_full_ref, cs_lanes_t_ref, cs_g_ref, cs_g_t_ref, field_ref, field_t_ref,
    spread_ref, spread_t_ref, cs_in_ref, cs_in_t_ref, flip_ref,
    resist_ref, new_free_ref, sums_ref,
    kern_s, half_s, field_s, bhalf_s, level_s, turned_s, sums_s,
):
    i = pl.program_id(0)
    j = pl.program_id(1)
    band = spectra_ref.shape[1]
    kernels = spectra_ref.shape[2]
    tile = target_ref.shape[0]
    pad_side = cs_full_ref.shape[1]
    pad_lanes = cs_lanes_t_ref.shape[0]
    grid = 2 * band
    blocks = grid // STRIP
    low = lambda v: v.astype(jnp.bfloat16)

    @pl.when((i == 0) & (j == 0))
    def _():
        sums_s[...] = jnp.zeros_like(sums_s)
        for k in range(kernels):
            weight = jnp.full((band, LANES), weights_ref[k], jnp.float32)
            scale = jnp.sqrt(weight) / (pad_side * band)
            for part in range(2):
                kern_s[part, k] = spectra_ref[part, :, k, :] * scale

    at_row = i * tile
    at_col = j * tile
    window = padded_ref[
        pl.ds(pl.multiple_of(at_row, 128), pad_side), pl.ds(pl.multiple_of(at_col, 128), pad_lanes)
    ]
    forw = low(dot(cs_full_ref[...], window))
    spec = dot(forw, cs_lanes_t_ref[...])
    spec_re = spec[:band, :band] + spec[band:, band:]
    spec_im = spec[band:, :band] - spec[:band, band:]
    for k in range(kernels):
        amp_re = low(kern_s[0, k] * spec_re - kern_s[1, k] * spec_im)
        amp_im = low(kern_s[0, k] * spec_im + kern_s[1, k] * spec_re)
        upper = jnp.concatenate([amp_re, amp_im], axis=1)
        lower = jnp.concatenate([-amp_im, amp_re], axis=1)
        half = low(dot(cs_g_t_ref[...], jnp.concatenate([upper, lower], axis=0)))
        half_s[:, k] = half.reshape(blocks, STRIP, grid)
    for b in range(0, blocks, GROUP):
        lines = half_s[b : b + GROUP].reshape(GROUP * kernels * STRIP, grid)
        field = dot(lines, field_ref[...])
        re = field[:, :grid]
        im = field[:, grid:]
        power = (re * re + im * im).reshape(GROUP, kernels, STRIP, grid)
        level_s[b : b + GROUP] = jnp.sum(power, axis=1)
        field_s[b : b + GROUP] = low(field).reshape(GROUP, kernels, STRIP, 2 * grid)
    level = level_s[...].reshape(grid, grid)
    mean = jnp.sum(jnp.sum(level, axis=0, keepdims=True), axis=1, keepdims=True) / (grid * grid)
    lines = low(dot(spread_ref[...], low(level - mean)))
    intensity = dot(lines, spread_t_ref[...]) + mean
    resist = jax.nn.sigmoid(resist_gain * (intensity - resist_level))
    resist_ref[...] = resist
    slopes = (4.0 * resist_gain) * (resist - target_ref[...]) * resist * (1.0 - resist)
    lines = low(dot(spread_t_ref[...], low(slopes)))
    level_s[...] = dot(lines, spread_ref[...]).reshape(blocks, STRIP, grid)
    for b in range(0, blocks, GROUP):
        pull = level_s[b : b + GROUP].reshape(GROUP, 1, STRIP, grid)
        pull = jnp.concatenate([pull, pull], axis=3)
        back = low(field_s[b : b + GROUP].astype(jnp.float32) * pull)
        bhalf = low(dot(back.reshape(GROUP * kernels * STRIP, 2 * grid), field_t_ref[...]))
        bhalf = bhalf.reshape(GROUP, kernels, STRIP, grid)
        for g in range(GROUP):
            bhalf_s[:, b + g] = bhalf[g]
    bspec_re = jnp.zeros((band, band), jnp.float32)
    bspec_im = jnp.zeros((band, band), jnp.float32)
    for k in range(kernels):
        bamp = dot(cs_g_ref[...], bhalf_s[k].reshape(grid, grid))
        bamp_re = bamp[:band, :band] + bamp[band:, band:]
        bamp_im = bamp[:band, band:] - bamp[band:, :band]
        bspec_re += kern_s[0, k] * bamp_re + kern_s[1, k] * bamp_im
        bspec_im += kern_s[0, k] * bamp_im - kern_s[1, k] * bamp_re
    upper = jnp.concatenate([low(bspec_re), low(-bspec_im)], axis=1)
    lower = jnp.concatenate([low(bspec_im), low(bspec_re)], axis=1)
    bforw = low(dot(jnp.concatenate([upper, lower], axis=0), cs_in_ref[...]))
    gradient = dot(cs_in_t_ref[...], bforw)
    shading = padded_ref[
        pl.ds(pl.multiple_of(at_row + HALO, HALO), tile), pl.ds(pl.multiple_of(at_col + LANES, LANES), tile)
    ].astype(jnp.float32)
    grad_param = gradient * (1.0 - shading * shading)
    new_free_ref[...] = free_ref[...] - step_free * grad_param
    turned_s[0] = grad_param
    plain = low(grad_param)
    group = flip_ref.shape[0]
    for at in range(0, tile, group):
        part = slice(at, at + group)
        across = dot(plain[:, part], flip_ref[...])
        turned_s[2, :, part] = across
        for f, source in ((1, plain[:, part]), (3, low(across))):
            for up in range(0, tile, group):
                turned_s[f, up : up + group, part] = dot(flip_ref[...], source[up : up + group])
    cells = tile // CELL
    left = left_mask(CELL)

    def cells_step(a, carry):
        rows = pl.ds(pl.multiple_of(a * CELL, CELL), CELL)
        for pair in range(cells // 2):
            s0, s1, o0, o1 = pair_codes(
                inst_ref, orient_ref, owner_ref, i * cells + a, j * cells + 2 * pair
            )
            lanes = slice(pair * LANES, (pair + 1) * LANES)
            sums_s[s0] += jnp.where(left, turned_s[o0, rows, lanes], 0.0)
            sums_s[s1] += jnp.where(left, 0.0, turned_s[o1, rows, lanes])
        return carry

    lax.fori_loop(0, cells, cells_step, 0)

    @pl.when((i == pl.num_programs(0) - 1) & (j == pl.num_programs(1) - 1))
    def _():
        def pack(p, carry):
            one = sums_s[2 * p]
            two = sums_s[2 * p + 1]
            one = one + pltpu.roll(one, CELL, 1)
            two = two + pltpu.roll(two, CELL, 1)
            sums_ref[p] = low(jnp.where(left, one, two))
            return carry

        lax.fori_loop(0, sums_ref.shape[0], pack, 0)


def tile_steps(inst, orient, owner, weights, padded, target, free, spectra, consts, flip, masters):
    height, width = target.shape
    band = spectra.shape[1]
    kernels = spectra.shape[2]
    grid = 2 * band
    blocks = grid // STRIP
    tile_spec = pl.BlockSpec((TILE, TILE), lambda i, j, *_: (i, j))
    sums_shape = (masters // 2, CELL, LANES)
    once = [padded, None, None, spectra, *consts, flip]
    return pl.pallas_call(
        tile_kernel,
        grid_spec=pltpu.PrefetchScalarGridSpec(
            num_scalar_prefetch=4,
            grid=(height // TILE, width // TILE),
            in_specs=[tile_spec if v is None else whole_spec(v) for v in once],
            out_specs=[tile_spec, tile_spec, pl.BlockSpec(sums_shape, lambda *_: (0, 0, 0))],
            scratch_shapes=[
                pltpu.VMEM((2, kernels, band, band), jnp.float32),
                pltpu.VMEM((blocks, kernels, STRIP, grid), jnp.bfloat16),
                pltpu.VMEM((blocks, kernels, STRIP, 2 * grid), jnp.bfloat16),
                pltpu.VMEM((kernels, blocks, STRIP, grid), jnp.bfloat16),
                pltpu.VMEM((blocks, STRIP, grid), jnp.float32),
                pltpu.VMEM((4, TILE, TILE), jnp.float32),
                pltpu.VMEM((masters, CELL, LANES), jnp.float32),
            ],
        ),
        out_shape=[
            jax.ShapeDtypeStruct(target.shape, jnp.float32),
            jax.ShapeDtypeStruct(target.shape, jnp.float32),
            jax.ShapeDtypeStruct(sums_shape, jnp.bfloat16),
        ],
        compiler_params=pltpu.CompilerParams(vmem_limit_bytes=60 * 1024 * 1024),
        name="tile_steps",
    )(inst, orient, owner, weights, padded, target, free, spectra, *consts, flip)


MESH = pl.DeviceIdType.MESH
VM = pl.BlockSpec(memory_space=pltpu.VMEM)


def split_id(flat, n_col):
    return (lax.div(flat, n_col), lax.rem(flat, n_col))


def greet(peers):
    barrier = pltpu.get_barrier_semaphore()
    for peer in peers:
        pl.semaphore_signal(barrier, inc=1, device_id=peer, device_id_type=MESH)
    pl.semaphore_wait(barrier, len(peers))


def level_peers(n_row, n_col):
    r = lax.axis_index("row")
    c = lax.axis_index("col")
    long = n_col // 2
    z, y = lax.div(c, 2), lax.rem(c, 2)
    x, core = lax.div(r, 2), lax.rem(r, 2)
    p = x * 2 + y

    def z_at(t):
        return lax.rem(z + t + long, long)

    def p_at(t):
        q = lax.rem(p + t + n_row, n_row)
        return lax.div(q, 2), lax.rem(q, 2)

    return r, c, z, y, x, core, long, z_at, p_at


def gather_ids(n_row, n_col):
    r, c, z, y, x, core, long, z_at, p_at = level_peers(n_row, n_col)
    ids = [(r, z_at(t) * 2 + y) for t in range(1, long)]
    for t in range(1, n_row):
        px, py = p_at(t)
        ids.append((px * 2 + core, z * 2 + py))
    return ids + [(x * 2 + 1 - core, c)]


def gather_levels(n_row, n_col, own, table_ref, stored, send_sem, recv_sem):
    r, c, z, y, x, core, long, z_at, p_at = level_peers(n_row, n_col)
    share = stored // n_row

    def block(row, col):
        return table_ref.at[pl.ds(col * stored + row * share, share)]

    def make(src, dst, level, at, peer):
        return pltpu.make_async_remote_copy(
            src_ref=src,
            dst_ref=dst,
            send_sem=send_sem.at[level, at],
            recv_sem=recv_sem.at[level, at],
            device_id=peer,
            device_id_type=MESH,
        )

    partner = (x * 2 + 1 - core, c)
    mine = block(r, c)
    first = [make(own, mine, 0, t, (r, z_at(t) * 2 + y)) for t in range(1, long)]
    for copy in first:
        copy.start()
    second = []
    third = []
    for t in range(long):
        if t > 0:
            first[t - 1].wait_recv()
        here = block(r, z_at(-t) * 2 + y)
        src = own if t == 0 else here
        for q in range(1, n_row):
            px, py = p_at(q)
            copy = make(src, here, 1, t * n_row + q, (px * 2 + core, z * 2 + py))
            copy.start()
            second.append(copy)
        copy = make(src, here, 2, t * n_row, partner)
        copy.start()
        third.append(copy)
    for t in range(long):
        for q in range(1, n_row):
            second[t * (n_row - 1) + q - 1].wait_recv()
            px, py = p_at(-q)
            here = block(px * 2 + core, z_at(-t) * 2 + py)
            copy = make(here, here, 2, t * n_row + q, partner)
            copy.start()
            third.append(copy)
    for copy in third:
        copy.wait_recv()
    for copy in first + second + third:
        copy.wait_send()


def gather_sems(n_row, n_col):
    shape = (3, n_row * n_col // 2)
    return [pltpu.SemaphoreType.DMA(shape), pltpu.SemaphoreType.DMA(shape)]


def gather_kernel(n_row, n_col, own_ref, table_ref, send_sem, recv_sem):
    r = lax.axis_index("row")
    c = lax.axis_index("col")
    stored = own_ref.shape[0]
    share = stored // n_row
    greet(gather_ids(n_row, n_col))
    own = own_ref.at[pl.ds(r * share, share)]
    table_ref[pl.ds(c * stored + r * share, share)] = own_ref[pl.ds(r * share, share)]
    gather_levels(n_row, n_col, own, table_ref, stored, send_sem, recv_sem)


def gather_masters(own, n_row, n_col):
    return pl.pallas_call(
        functools.partial(gather_kernel, n_row, n_col),
        in_specs=[VM],
        out_specs=VM,
        out_shape=jax.ShapeDtypeStruct((n_col * own.shape[0],) + own.shape[1:], own.dtype),
        scratch_shapes=gather_sems(n_row, n_col),
        compiler_params=pltpu.CompilerParams(collective_id=0, has_side_effects=True),
        name="gather_masters",
    )(own)


def halo_kernel(
    n_row, n_col, mask_ref, edge_l_ref, edge_r_ref, out_ref, from_l, from_r, send_sem, recv_sem
):
    r = lax.axis_index("row")
    c = lax.axis_index("col")
    height, width = mask_ref.shape
    packed = height // 2
    middle = slice(LANES, LANES + width)
    row_parts = {
        -1: (slice(0, HALO), slice(HALO + height, 2 * HALO + height)),
        1: (slice(height - HALO, height), slice(0, HALO)),
    }
    edge_parts = {
        -1: (slice(0, HALF), slice(HALF + packed, 2 * HALF + packed)),
        0: (slice(0, packed), slice(HALF, HALF + packed)),
        1: (slice(packed - HALF, packed), slice(0, HALF)),
    }
    moves = [(0, 1), (0, -1), (1, 0), (-1, 0), (1, 1), (1, -1), (-1, 1), (-1, -1)]
    ids = [(lax.rem(r + n_row + dr, n_row), lax.rem(c + n_col + dc, n_col)) for dr, dc in moves]

    def inside(dr, dc):
        return (r + dr >= 0) & (r + dr < n_row) & (c + dc >= 0) & (c + dc < n_col)

    work = []
    for at, (dr, dc) in enumerate(moves):
        if dc == 0:
            src, dst = row_parts[dr]
            src, dst = mask_ref.at[src], out_ref.at[dst, middle]
        else:
            src, dst = edge_parts[dr]
            src = (edge_r_ref if dc == 1 else edge_l_ref).at[src]
            dst = (from_l if dc == 1 else from_r).at[dst]
        copy = pltpu.make_async_remote_copy(
            src_ref=src,
            dst_ref=dst,
            send_sem=send_sem.at[at],
            recv_sem=recv_sem.at[at],
            device_id=ids[at],
            device_id_type=MESH,
        )
        work.append((copy, dst, inside(dr, dc), inside(-dr, -dc)))
    greet(ids)
    for copy, dst, sends, gets in work:
        pl.when(sends)(copy.start)
    for copy, dst, sends, gets in work:

        @pl.when(jnp.logical_not(gets))
        def _():
            dst[...] = jnp.zeros(dst.shape, dst.dtype)

    out_ref[HALO : HALO + height, middle] = mask_ref[...]
    for copy, dst, sends, gets in work:
        pl.when(gets)(copy.wait_recv)
    left = left_mask(HALF)

    def unpack(a, carry):
        rows = pl.ds(pl.multiple_of(a * HALF, HALF), HALF)
        upper = pl.ds(pl.multiple_of(a * CELL, CELL), HALF)
        lower = pl.ds(pl.multiple_of(a * CELL + HALF, HALF), HALF)
        one = from_l[rows].astype(jnp.float32)
        two = from_r[rows].astype(jnp.float32)
        cast = lambda v: v.astype(jnp.bfloat16)
        last = slice(LANES + width, 2 * LANES + width)
        out_ref[upper, :LANES] = cast(jnp.where(left, 0.0, pltpu.roll(one, CELL, 1)))
        out_ref[lower, :LANES] = cast(jnp.where(left, 0.0, one))
        out_ref[upper, last] = cast(jnp.where(left, two, 0.0))
        out_ref[lower, last] = cast(jnp.where(left, pltpu.roll(two, CELL, 1), 0.0))
        return carry

    lax.fori_loop(0, (height + 2 * HALO) // CELL, unpack, 0)
    for copy, dst, sends, gets in work:
        pl.when(sends)(copy.wait_send)


def with_halo(mask, edge_l, edge_r, n_row, n_col):
    height, width = mask.shape
    return pl.pallas_call(
        functools.partial(halo_kernel, n_row, n_col),
        in_specs=[VM, VM, VM],
        out_specs=VM,
        out_shape=jax.ShapeDtypeStruct((height + 2 * HALO, width + 2 * LANES), mask.dtype),
        scratch_shapes=[
            pltpu.VMEM((height // 2 + 2 * HALF, LANES), mask.dtype),
            pltpu.VMEM((height // 2 + 2 * HALF, LANES), mask.dtype),
            pltpu.SemaphoreType.DMA((8,)),
            pltpu.SemaphoreType.DMA((8,)),
        ],
        compiler_params=pltpu.CompilerParams(collective_id=1, has_side_effects=True),
        name="with_halo",
    )(mask, edge_l, edge_r)


def smooth_packed(cells):
    count = cells.shape[0]
    flat = cells.reshape(count * CELL, LANES)
    x = lax.broadcasted_iota(jnp.int32, flat.shape, 1) % CELL
    y = lax.broadcasted_iota(jnp.int32, flat.shape, 0) % CELL
    before = jnp.where(x == 0, 0.0, pltpu.roll(flat, 1, 1))
    after = jnp.where(x == CELL - 1, 0.0, pltpu.roll(flat, LANES - 1, 1))
    up = jnp.where(y == 0, 0.0, pltpu.roll(flat, 1, 0))
    down = jnp.where(y == CELL - 1, 0.0, pltpu.roll(flat, count * CELL - 1, 0))
    return (0.5 * flat + 0.125 * (before + after + up + down)).reshape(cells.shape)


def update_kernel(
    n_row, n_col, sums_ref, own_ref, table_ref,
    parts, fresh, send_sem, recv_sem, send2_sem, recv2_sem,
):
    r = lax.axis_index("row")
    c = lax.axis_index("col")
    count = n_row * n_col
    me = r * n_col + c
    stored = own_ref.shape[0]
    share = stored // n_row
    barrier = pltpu.get_barrier_semaphore()

    def first_row(flat):
        pr, pc = split_id(flat, n_col)
        return pc * stored + pr * share

    def hello(t, carry):
        pl.semaphore_signal(
            barrier, inc=1, device_id=split_id(lax.rem(me + t, count), n_col), device_id_type=MESH
        )
        return carry

    lax.fori_loop(1, count, hello, 0)
    pl.semaphore_wait(barrier, count - 1)

    def part_copy(t):
        peer = lax.rem(me + t, count)
        return pltpu.make_async_remote_copy(
            src_ref=sums_ref.at[pl.ds(first_row(peer), share)],
            dst_ref=parts.at[t],
            send_sem=send_sem.at[t],
            recv_sem=recv_sem.at[t],
            device_id=split_id(peer, n_col),
            device_id_type=MESH,
        )

    def start_part(t, carry):
        part_copy(t).start()
        return carry

    lax.fori_loop(1, count, start_part, 0)

    def add_part(t, total):
        part_copy(t).wait_recv()
        return total + parts[t].astype(jnp.float32)

    mine = first_row(me)
    total = lax.fori_loop(1, count, add_part, sums_ref[pl.ds(mine, share)].astype(jnp.float32))
    updated = own_ref[pl.ds(r * share, share)] - step_master * total
    value = smooth_packed(updated).astype(jnp.bfloat16)
    fresh[...] = value
    table_ref[pl.ds(mine, share)] = value

    def end_part(t, carry):
        part_copy(t).wait_send()
        return carry

    lax.fori_loop(1, count, end_part, 0)

    gather_levels(n_row, n_col, fresh, table_ref, stored, send2_sem, recv2_sem)


def update_masters(sums, own, n_row, n_col):
    count = n_row * n_col
    piece = (own.shape[0] // n_row,) + own.shape[1:]
    return pl.pallas_call(
        functools.partial(update_kernel, n_row, n_col),
        in_specs=[VM, VM],
        out_specs=VM,
        out_shape=jax.ShapeDtypeStruct(sums.shape, jnp.bfloat16),
        scratch_shapes=[
            pltpu.VMEM((count,) + piece, jnp.bfloat16),
            pltpu.VMEM(piece, jnp.bfloat16),
            pltpu.SemaphoreType.DMA((count,)),
            pltpu.SemaphoreType.DMA((count,)),
            *gather_sems(n_row, n_col),
        ],
        compiler_params=pltpu.CompilerParams(collective_id=2, has_side_effects=True),
        name="update_masters",
    )(sums, own)


def per_device(
    masters, inst_master, inst_orient, owner_map, tile_free, target, kernel_spectra, socs_weights
):
    stored = masters.shape[0] // 2
    total = owner_map.shape[0]
    consts = tables(TILE + 2 * HALO, kernel_spectra.shape[1], HALO, TILE)
    flip, spread = flips()
    own = masters.reshape(stored, 2, CELL, CELL).transpose(0, 2, 1, 3).reshape(stored, CELL, LANES)
    n_row = lax.axis_size("row")
    n_col = lax.axis_size("col")
    table = gather_masters(own.astype(jnp.bfloat16), n_row, n_col)
    mask, edge_l, edge_r = image(
        inst_master, inst_orient, owner_map, table, tile_free, flip, spread, True
    )
    padded = with_halo(mask, edge_l, edge_r, n_row, n_col)
    resist, new_free, sums = tile_steps(
        inst_master, inst_orient, owner_map, socs_weights, padded, target, tile_free,
        kernel_spectra, consts, flip, total,
    )
    table = update_masters(sums, own, n_row, n_col)
    fresh = lax.dynamic_slice_in_dim(table, lax.axis_index("col") * stored, stored, 0)
    (new_mask,) = image(
        inst_master, inst_orient, owner_map, table, new_free, flip, spread, False
    )
    fresh = fresh.astype(jnp.float32).reshape(stored, CELL, 2, CELL).transpose(0, 2, 1, 3)
    return (resist, new_mask, fresh.reshape(masters.shape))


def solution(mesh):
    in_specs = (
        P("col", None),
        P("row", "col"),
        P("row", "col"),
        P(),
        P("row", "col"),
        P("row", "col"),
        P(),
        P(),
    )
    out_specs = (P("row", "col"), P("row", "col"), P("col", None))
    return jax.shard_map(
        per_device, mesh=mesh, in_specs=in_specs, out_specs=out_specs, check_vma=False
    )
```

```python
import functools
import math

import jax
import jax.numpy as jnp
import numpy as np
from jax import lax
from jax.experimental import pallas as pl
from jax.experimental.pallas import tpu as pltpu
from jax.sharding import PartitionSpec as P

TILE = 512
TPD = 2
HALO = 64
CELL = 64
LANES = 128
HALF = CELL // 2
STRIP = 16
GROUP = 4
SLAB = 256
VM = pl.BlockSpec(memory_space=pltpu.VMEM)
MESH = pl.DeviceIdType.MESH
GAIN_GRID = 1.9925
GAIN_SPREAD = 1.725625

step_free = 1.0
step_master = 0.05
resist_gain = 2.0
resist_level = 1.8


def dot(left, right):
    return jnp.dot(left, right, preferred_element_type=jnp.float32)


def bfloat(value):
    return jnp.asarray(np.ascontiguousarray(value).astype(jnp.bfloat16))


def tables(pad_side, band_side, halo, tile):
    freqs = np.arange(band_side, dtype=np.int64) - band_side // 2
    phases = (freqs[:, None] * np.arange(pad_side)[None, :]) % pad_side
    angles = phases.astype(np.float32) * np.float32(2.0 * math.pi / pad_side)
    cos = np.cos(angles)
    sin = np.sin(angles)
    cos_in = cos[:, halo : halo + tile]
    sin_in = sin[:, halo : halo + tile]
    cs_full = np.concatenate([cos, sin], 0)
    cs_lanes = np.pad(cs_full, ((0, 0), (LANES - halo, LANES - halo)))
    cs_in = np.concatenate([cos_in, sin_in], 0)
    grid = 2 * band_side
    turns = (freqs[:, None] * np.arange(grid)[None, :]) % grid
    cos_g = GAIN_GRID * np.cos(turns * (2.0 * math.pi / grid))
    sin_g = GAIN_GRID * np.sin(turns * (2.0 * math.pi / grid))
    cs_g = np.concatenate([cos_g, sin_g], 0)
    field = np.block([[cos_g, sin_g], [-sin_g, cos_g]])
    gaps = np.arange(halo, halo + tile)[:, None] / pad_side - np.arange(grid)[None, :] / grid
    waves = np.arange(1, band_side)
    spread = (1.0 + 2.0 * np.cos(2.0 * math.pi * gaps[:, :, None] * waves).sum(-1)) * (GAIN_SPREAD / grid)
    parts = (cs_full, cs_lanes.T, cs_g, cs_g.T, field, field.T, spread, spread.T, cs_in, cs_in.T)
    return [bfloat(p) for p in parts]


def flips():
    back = np.eye(CELL)[::-1]
    rows = np.kron(np.eye(4), back)
    same = np.eye(CELL)
    none = np.zeros((CELL, CELL))
    spread = [
        np.block([[m, m], [none, none]]) if e == 0 else np.block([[none, none], [m, m]])
        for m in (same, back)
        for e in range(2)
    ]
    return bfloat(rows), bfloat(np.concatenate(spread, 1))


def left_mask(rows):
    return lax.broadcasted_iota(jnp.int32, (rows, LANES), 1) < CELL


def pair_codes(inst_ref, orient_ref, owner_ref, a, b):
    s0 = owner_ref[inst_ref[a, b]]
    s1 = owner_ref[inst_ref[a, b + 1]]
    return s0, s1, orient_ref[a, b], orient_ref[a, b + 1]


def turn_block(table_ref, turned_ref, flip_ref, spread_ref, at, count):
    total = turned_ref.shape[0] // 4
    rows = count * CELL
    cells = table_ref[pl.ds(at, count)].reshape(rows, LANES)
    flipped = dot(flip_ref[:rows, :rows], cells).astype(jnp.bfloat16)
    both = dot(jnp.concatenate([cells, flipped], axis=0), spread_ref[...]).astype(jnp.bfloat16)
    for f in range(2):
        for c in range(2):
            for e in range(2):
                lanes = slice((2 * c + e) * LANES, (2 * c + e + 1) * LANES)
                for p in range(count):
                    start = f * rows + p * CELL
                    turned_ref[(2 * c + f) * total + 2 * (at + p) + e] = both[start : start + CELL, lanes]


def assemble_pair(turned_ref, codes):
    s0, s1, o0, o1 = codes
    total = turned_ref.shape[0] // 4
    one = turned_ref[o0 * total + s0].astype(jnp.float32)
    two = turned_ref[o1 * total + s1].astype(jnp.float32)
    return jnp.where(left_mask(CELL), one, two)


def image_kernel(inst_ref, orient_ref, owner_ref, turned_ref, free_ref, out_ref):
    steps = free_ref.shape[0] // CELL
    first = pl.program_id(0) * steps

    def step(a, carry):
        rows = pl.ds(pl.multiple_of(a * CELL, CELL), CELL)
        for pair in range(free_ref.shape[1] // LANES):
            codes = pair_codes(inst_ref, orient_ref, owner_ref, first + a, 2 * pair)
            cells = assemble_pair(turned_ref, codes)
            lanes = slice(pair * LANES, (pair + 1) * LANES)
            out_ref[rows, lanes] = jnp.tanh(cells + free_ref[rows, lanes])
        return carry

    lax.fori_loop(0, steps, step, 0)


def whole_spec(array):
    zeros = (0,) * array.ndim
    return pl.BlockSpec(array.shape, lambda *_: zeros)


def image(inst, orient, owner, turned, free):
    height, width = free.shape
    strip = pl.BlockSpec((SLAB, width), lambda a, *_: (a, 0))
    return pl.pallas_call(
        image_kernel,
        grid_spec=pltpu.PrefetchScalarGridSpec(
            num_scalar_prefetch=3,
            grid=(height // SLAB,),
            in_specs=[VM, strip],
            out_specs=strip,
        ),
        out_shape=jax.ShapeDtypeStruct(free.shape, jnp.float32),
        compiler_params=pltpu.CompilerParams(vmem_limit_bytes=8 * 1024 * 1024),
        name="image",
    )(inst, orient, owner, turned, free)


def tile_kernel(
    n_row, n_col, inst_ref, orient_ref, owner_ref, weights_ref,
    padded_ref, target_ref, free_ref, spectra_ref,
    cs_full_ref, cs_lanes_t_ref, cs_g_ref, cs_g_t_ref, field_ref, field_t_ref,
    spread_ref, spread_t_ref, cs_in_ref, cs_in_t_ref, flip_ref,
    resist_ref, new_free_ref, sums_ref,
    kern_s, half_s, field_s, bhalf_s, level_s, turned_s, sums_s,
):
    i = pl.program_id(0)
    j = pl.program_id(1)
    band = spectra_ref.shape[1]
    kernels = spectra_ref.shape[2]
    tile = target_ref.shape[0]
    pad_side = cs_full_ref.shape[1]
    pad_lanes = cs_lanes_t_ref.shape[0]
    grid = 2 * band
    blocks = grid // STRIP
    low = lambda v: v.astype(jnp.bfloat16)

    @pl.when((i == 0) & (j == 0))
    def _():
        sums_s[...] = jnp.zeros_like(sums_s)
        for k in range(kernels):
            weight = jnp.full((band, LANES), weights_ref[k], jnp.float32)
            scale = jnp.sqrt(weight) / (pad_side * band * GAIN_GRID**2)
            for part in range(2):
                kern_s[part, k] = spectra_ref[part, :, k, :] * scale

    at_row = i * tile
    at_col = j * tile
    window = padded_ref[
        pl.ds(pl.multiple_of(at_row, 128), pad_side), pl.ds(pl.multiple_of(at_col, 128), pad_lanes)
    ]
    forw = low(dot(cs_full_ref[...], window))
    spec = dot(forw, cs_lanes_t_ref[...])
    spec_re = spec[:band, :band] + spec[band:, band:]
    spec_im = spec[band:, :band] - spec[:band, band:]
    for k in range(kernels):
        amp_re = low(kern_s[0, k] * spec_re - kern_s[1, k] * spec_im)
        amp_im = low(kern_s[0, k] * spec_im + kern_s[1, k] * spec_re)
        upper = jnp.concatenate([amp_re, amp_im], axis=1)
        lower = jnp.concatenate([-amp_im, amp_re], axis=1)
        half = low(dot(cs_g_t_ref[...], jnp.concatenate([upper, lower], axis=0)))
        half_s[:, k] = half.reshape(blocks, STRIP, grid)
    for b in range(0, blocks, GROUP):
        lines = half_s[b : b + GROUP].reshape(GROUP * kernels * STRIP, grid)
        field = dot(lines, field_ref[...])
        re = field[:, :grid]
        im = field[:, grid:]
        power = (re * re + im * im).reshape(GROUP, kernels, STRIP, grid)
        level_s[b : b + GROUP] = jnp.sum(power, axis=1)
        field_s[b : b + GROUP] = low(field).reshape(GROUP, kernels, STRIP, 2 * grid)
    level = level_s[...].reshape(grid, grid)
    mean = jnp.sum(jnp.sum(level, axis=0, keepdims=True), axis=1, keepdims=True) / (grid * grid)
    lines = low(dot(spread_ref[...], low(level - mean)))
    intensity = dot(lines, spread_t_ref[...]) * (1.0 / GAIN_SPREAD**2) + mean
    resist = jax.nn.sigmoid(resist_gain * (intensity - resist_level))
    resist_ref[...] = resist
    slopes = (4.0 * resist_gain / GAIN_SPREAD**2) * (resist - target_ref[...]) * resist * (1.0 - resist)
    lines = low(dot(spread_t_ref[...], low(slopes)))
    level_s[...] = dot(lines, spread_ref[...]).reshape(blocks, STRIP, grid)
    for b in range(0, blocks, GROUP):
        pull = level_s[b : b + GROUP].reshape(GROUP, 1, STRIP, grid)
        pull = jnp.concatenate([pull, pull], axis=3)
        back = low(field_s[b : b + GROUP].astype(jnp.float32) * pull)
        bhalf = low(dot(back.reshape(GROUP * kernels * STRIP, 2 * grid), field_t_ref[...]))
        bhalf = bhalf.reshape(GROUP, kernels, STRIP, grid)
        for g in range(GROUP):
            bhalf_s[:, b + g] = bhalf[g]
    bspec_re = jnp.zeros((band, band), jnp.float32)
    bspec_im = jnp.zeros((band, band), jnp.float32)
    for k in range(kernels):
        bamp = dot(cs_g_ref[...], bhalf_s[k].reshape(grid, grid))
        bamp_re = bamp[:band, :band] + bamp[band:, band:]
        bamp_im = bamp[:band, band:] - bamp[band:, :band]
        bspec_re += kern_s[0, k] * bamp_re + kern_s[1, k] * bamp_im
        bspec_im += kern_s[0, k] * bamp_im - kern_s[1, k] * bamp_re
    upper = jnp.concatenate([low(bspec_re), low(-bspec_im)], axis=1)
    lower = jnp.concatenate([low(bspec_im), low(bspec_re)], axis=1)
    bforw = low(dot(jnp.concatenate([upper, lower], axis=0), cs_in_ref[...]))
    gradient = dot(cs_in_t_ref[...], bforw)
    shading = padded_ref[
        pl.ds(pl.multiple_of(at_row + HALO, HALO), tile), pl.ds(pl.multiple_of(at_col + LANES, LANES), tile)
    ].astype(jnp.float32)
    grad_param = gradient * (1.0 - shading * shading)
    new_free_ref[...] = free_ref[...] - step_free * grad_param
    turned_s[0] = grad_param
    plain = low(grad_param)
    group = flip_ref.shape[0]
    for at in range(0, tile, group):
        part = slice(at, at + group)
        across = dot(plain[:, part], flip_ref[...])
        turned_s[2, :, part] = across
        for f, source in ((1, plain[:, part]), (3, low(across))):
            for up in range(0, tile, group):
                turned_s[f, up : up + group, part] = dot(flip_ref[...], source[up : up + group])
    cells = tile // CELL
    left = left_mask(CELL)

    def cells_step(a, carry):
        rows = pl.ds(pl.multiple_of(a * CELL, CELL), CELL)
        for pair in range(cells // 2):
            s0, s1, o0, o1 = pair_codes(
                inst_ref, orient_ref, owner_ref, i * cells + a, j * cells + 2 * pair
            )
            lanes = slice(pair * LANES, (pair + 1) * LANES)
            sums_s[s0] += jnp.where(left, turned_s[o0, rows, lanes], 0.0)
            sums_s[s1] += jnp.where(left, 0.0, turned_s[o1, rows, lanes])
        return carry

    lax.fori_loop(0, cells, cells_step, 0)

    @pl.when((i == pl.num_programs(0) - 1) & (j == pl.num_programs(1) - 1))
    def _():
        stored = sums_ref.shape[0] // n_col
        share = stored // n_row

        def pack(p, carry):
            one = sums_s[2 * p]
            two = sums_s[2 * p + 1]
            one = one + pltpu.roll(one, CELL, 1)
            two = two + pltpu.roll(two, CELL, 1)
            col = p // stored
            row = p % stored // share
            side = row % 2 * (n_col // 2) + col // 2
            spot = (side * n_row + row // 2 * 2 + col % 2) * share + p % share
            sums_ref[spot] = low(jnp.where(left, one, two))
            return carry

        lax.fori_loop(0, sums_ref.shape[0], pack, 0)


def tile_steps(inst, orient, owner, weights, padded, target, free, spectra, consts, flip, masters, n_row, n_col):
    height, width = target.shape
    band = spectra.shape[1]
    kernels = spectra.shape[2]
    grid = 2 * band
    blocks = grid // STRIP
    tile_spec = pl.BlockSpec((TILE, TILE), lambda i, j, *_: (i, j))
    sums_shape = (masters // 2, CELL, LANES)
    once = [padded, None, None, spectra, *consts, flip]
    return pl.pallas_call(
        functools.partial(tile_kernel, n_row, n_col),
        grid_spec=pltpu.PrefetchScalarGridSpec(
            num_scalar_prefetch=4,
            grid=(height // TILE, width // TILE),
            in_specs=[tile_spec if v is None else whole_spec(v) for v in once],
            out_specs=[tile_spec, tile_spec, pl.BlockSpec(sums_shape, lambda *_: (0, 0, 0))],
            scratch_shapes=[
                pltpu.VMEM((2, kernels, band, band), jnp.float32),
                pltpu.VMEM((blocks, kernels, STRIP, grid), jnp.bfloat16),
                pltpu.VMEM((blocks, kernels, STRIP, 2 * grid), jnp.bfloat16),
                pltpu.VMEM((kernels, blocks, STRIP, grid), jnp.bfloat16),
                pltpu.VMEM((blocks, STRIP, grid), jnp.float32),
                pltpu.VMEM((4, TILE, TILE), jnp.float32),
                pltpu.VMEM((masters, CELL, LANES), jnp.float32),
            ],
        ),
        out_shape=[
            jax.ShapeDtypeStruct(target.shape, jnp.float32),
            jax.ShapeDtypeStruct(target.shape, jnp.float32),
            jax.ShapeDtypeStruct(sums_shape, jnp.bfloat16),
        ],
        compiler_params=pltpu.CompilerParams(vmem_limit_bytes=60 * 1024 * 1024),
        name="tile_steps",
    )(inst, orient, owner, weights, padded, target, free, spectra, *consts, flip)


def greet(peers):
    barrier = pltpu.get_barrier_semaphore()
    for peer in peers:
        pl.semaphore_signal(barrier, inc=1, device_id=peer, device_id_type=MESH)
    pl.semaphore_wait(barrier, len(peers))


def level_peers(n_row, n_col):
    r = lax.axis_index("row")
    c = lax.axis_index("col")
    long = n_col // 2
    z, y = lax.div(c, 2), lax.rem(c, 2)
    x, core = lax.div(r, 2), lax.rem(r, 2)
    p = x * 2 + y

    def z_at(t):
        return lax.rem(z + t + long, long)

    def p_at(t):
        q = lax.rem(p + t + n_row, n_row)
        return lax.div(q, 2), lax.rem(q, 2)

    return r, c, z, y, x, core, long, z_at, p_at


def gather_ids(n_row, n_col):
    r, c, z, y, x, core, long, z_at, p_at = level_peers(n_row, n_col)
    ids = [(r, z_at(t) * 2 + y) for t in range(1, long)]
    for t in range(1, n_row):
        px, py = p_at(t)
        ids.append((px * 2 + core, z * 2 + py))
    return ids + [(x * 2 + 1 - core, c)]


def gather_levels(n_row, n_col, own, table_ref, stored, send_sem, recv_sem, ready):
    r, c, z, y, x, core, long, z_at, p_at = level_peers(n_row, n_col)
    share = stored // n_row
    partner = (x * 2 + 1 - core, c)

    def first_row(row, col):
        return col * stored + row * share

    def make(src, at, level, slot, peer):
        return pltpu.make_async_remote_copy(
            src_ref=src,
            dst_ref=table_ref.at[pl.ds(at, share)],
            send_sem=send_sem.at[level, slot],
            recv_sem=recv_sem.at[level, slot],
            device_id=peer,
            device_id_type=MESH,
        )

    def here(at):
        return table_ref.at[pl.ds(at, share)]

    mine = first_row(r, c)
    first = [make(own, mine, 0, t, (r, z_at(t) * 2 + y)) for t in range(1, long)]
    for copy in first:
        copy.start()
    second = []
    third = []
    for t in range(long):
        if t > 0:
            first[t - 1].wait_recv()
        at = first_row(r, z_at(-t) * 2 + y)
        src = own if t == 0 else here(at)
        for q in range(1, n_row):
            px, py = p_at(q)
            copy = make(src, at, 1, t * n_row + q, (px * 2 + core, z * 2 + py))
            copy.start()
            second.append(copy)
        copy = make(src, at, 2, t * n_row, partner)
        copy.start()
        third.append(copy)
    for t in range(long):
        ready(first_row(r, z_at(-t) * 2 + y))

    def across(n, carry):
        t = n // (n_row - 1)
        q = n % (n_row - 1) + 1
        slot = t * n_row + q
        px, py = p_at(-q)
        at = first_row(px * 2 + core, z_at(-t) * 2 + py)
        make(here(at), at, 1, slot, partner).wait_recv()
        make(here(at), at, 2, slot, partner).start()
        ready(at)
        return carry

    def beside(n, carry):
        t = n // n_row
        q = n % n_row
        px, py = p_at(-q)
        at = first_row(px * 2 + 1 - core, z_at(-t) * 2 + py)
        make(here(at), at, 2, n, partner).wait_recv()
        ready(at)
        return carry

    def sent(n, carry):
        make(here(mine), mine, 2, n, partner).wait_send()
        return carry

    lax.fori_loop(0, long * (n_row - 1), across, 0)
    lax.fori_loop(0, long * n_row, beside, 0)
    for copy in first + second:
        copy.wait_send()
    lax.fori_loop(0, long * n_row, sent, 0)


def gather_sems(n_row, n_col):
    shape = (3, n_row * n_col // 2)
    return [pltpu.SemaphoreType.DMA(shape), pltpu.SemaphoreType.DMA(shape)]


def front_kernel(
    n_row, n_col, inst_ref, orient_ref, owner_ref, own_ref, free_ref, flip_ref, spread_ref, out_ref,
    table_s, turned_s, free_s, edge_l, edge_r, from_l, from_r,
    free_sem, send_sem, recv_sem, halo_send, halo_recv,
):
    r = lax.axis_index("row")
    c = lax.axis_index("col")
    height, width = free_s.shape
    packed = height // 2
    stored = own_ref.shape[0]
    share = stored // n_row
    load_free = pltpu.make_async_copy(free_ref, free_s, free_sem)
    load_free.start()
    moves = [(0, 1), (0, -1), (1, 0), (-1, 0), (1, 1), (1, -1), (-1, 1), (-1, -1)]
    ids = [(lax.rem(r + n_row + dr, n_row), lax.rem(c + n_col + dc, n_col)) for dr, dc in moves]
    greet(gather_ids(n_row, n_col) + ids)
    own = own_ref.at[pl.ds(r * share, share)]
    table_s[pl.ds(c * stored + r * share, share)] = own_ref[pl.ds(r * share, share)]

    def ready(at):
        turn_block(table_s, turned_s, flip_ref, spread_ref, at, share)

    gather_levels(n_row, n_col, own, table_s, stored, send_sem, recv_sem, ready)
    load_free.wait()

    pairs = width // LANES
    strips = height // CELL
    cast = lambda v: v.astype(jnp.bfloat16)
    left = left_mask(HALF)

    def draw(a, pair):
        codes = pair_codes(inst_ref, orient_ref, owner_ref, a, 2 * pair)
        cells = assemble_pair(turned_s, codes)
        rows = pl.ds(pl.multiple_of(a * CELL, CELL), CELL)
        value = jnp.tanh(cells + free_s[rows, pair * LANES : (pair + 1) * LANES])
        rows = pl.ds(pl.multiple_of(HALO + a * CELL, CELL), CELL)
        out_ref[rows, (pair + 1) * LANES : (pair + 2) * LANES] = cast(value)
        return value

    def outer(n, carry):
        for pair in range(1, pairs - 1):
            draw(n * (strips - 1), pair)
        return carry

    def sides(a, carry):
        rows = pl.ds(pl.multiple_of(a * HALF, HALF), HALF)
        value = draw(a, 0)
        edge_l[rows] = cast(jnp.where(left, value[:HALF], pltpu.roll(value[HALF:], CELL, 1)))
        value = draw(a, pairs - 1)
        edge_r[rows] = cast(jnp.where(left, pltpu.roll(value[:HALF], CELL, 1), value[HALF:]))
        return carry

    def inner(a, carry):
        for pair in range(1, pairs - 1):
            draw(a, pair)
        return carry

    lax.fori_loop(0, 2, outer, 0)
    lax.fori_loop(0, strips, sides, 0)
    lax.fori_loop(1, 3, inner, 0)

    middle = slice(LANES, LANES + width)
    row_parts = {
        -1: (slice(HALO, 2 * HALO), slice(HALO + height, 2 * HALO + height)),
        1: (slice(height, HALO + height), slice(0, HALO)),
    }
    edge_parts = {
        -1: (slice(0, HALF), slice(HALF + packed, 2 * HALF + packed)),
        0: (slice(0, packed), slice(HALF, HALF + packed)),
        1: (slice(packed - HALF, packed), slice(0, HALF)),
    }

    def inside(dr, dc):
        return (r + dr >= 0) & (r + dr < n_row) & (c + dc >= 0) & (c + dc < n_col)

    work = []
    for at, (dr, dc) in enumerate(moves):
        if dc == 0:
            src, dst = row_parts[dr]
            src, dst = out_ref.at[src, middle], out_ref.at[dst, middle]
        else:
            src, dst = edge_parts[dr]
            src = (edge_r if dc == 1 else edge_l).at[src]
            dst = (from_l if dc == 1 else from_r).at[dst]
        copy = pltpu.make_async_remote_copy(
            src_ref=src,
            dst_ref=dst,
            send_sem=halo_send.at[at],
            recv_sem=halo_recv.at[at],
            device_id=ids[at],
            device_id_type=MESH,
        )
        work.append((copy, dst, inside(dr, dc), inside(-dr, -dc)))
    for copy, dst, sends, gets in work:
        pl.when(sends)(copy.start)
    lax.fori_loop(3, strips - 1, inner, 0)
    for copy, dst, sends, gets in work:

        @pl.when(jnp.logical_not(gets))
        def _():
            dst[...] = jnp.zeros(dst.shape, dst.dtype)

    for copy, dst, sends, gets in work:
        pl.when(gets)(copy.wait_recv)

    def unpack(a, carry):
        rows = pl.ds(pl.multiple_of(a * HALF, HALF), HALF)
        upper = pl.ds(pl.multiple_of(a * CELL, CELL), HALF)
        lower = pl.ds(pl.multiple_of(a * CELL + HALF, HALF), HALF)
        one = from_l[rows].astype(jnp.float32)
        two = from_r[rows].astype(jnp.float32)
        last = slice(LANES + width, 2 * LANES + width)
        out_ref[upper, :LANES] = cast(jnp.where(left, 0.0, pltpu.roll(one, CELL, 1)))
        out_ref[lower, :LANES] = cast(jnp.where(left, 0.0, one))
        out_ref[upper, last] = cast(jnp.where(left, two, 0.0))
        out_ref[lower, last] = cast(jnp.where(left, pltpu.roll(two, CELL, 1), 0.0))
        return carry

    lax.fori_loop(0, (height + 2 * HALO) // CELL, unpack, 0)
    for copy, dst, sends, gets in work:
        pl.when(sends)(copy.wait_send)


def front(inst, orient, owner, own, free, flip, spread, n_row, n_col):
    height, width = free.shape
    smem = pl.BlockSpec(memory_space=pltpu.SMEM)
    low = jnp.bfloat16
    pairs = n_col * own.shape[0]
    return pl.pallas_call(
        functools.partial(front_kernel, n_row, n_col),
        in_specs=[smem, smem, smem, VM, pl.BlockSpec(memory_space=pl.ANY), VM, VM],
        out_specs=VM,
        out_shape=jax.ShapeDtypeStruct((height + 2 * HALO, width + 2 * LANES), low),
        scratch_shapes=[
            pltpu.VMEM((pairs, CELL, LANES), low),
            pltpu.VMEM((8 * pairs, CELL, LANES), low),
            pltpu.VMEM((height, width), jnp.float32),
            pltpu.VMEM((height // 2, LANES), low),
            pltpu.VMEM((height // 2, LANES), low),
            pltpu.VMEM((height // 2 + 2 * HALF, LANES), low),
            pltpu.VMEM((height // 2 + 2 * HALF, LANES), low),
            pltpu.SemaphoreType.DMA,
            *gather_sems(n_row, n_col),
            pltpu.SemaphoreType.DMA((8,)),
            pltpu.SemaphoreType.DMA((8,)),
        ],
        compiler_params=pltpu.CompilerParams(
            collective_id=0, has_side_effects=True, vmem_limit_bytes=40 * 1024 * 1024
        ),
        name="front",
    )(inst, orient, owner, own, free, flip, spread)


def smooth_packed(cells):
    count = cells.shape[0]
    flat = cells.reshape(count * CELL, LANES)
    x = lax.broadcasted_iota(jnp.int32, flat.shape, 1) % CELL
    y = lax.broadcasted_iota(jnp.int32, flat.shape, 0) % CELL
    before = jnp.where(x == 0, 0.0, pltpu.roll(flat, 1, 1))
    after = jnp.where(x == CELL - 1, 0.0, pltpu.roll(flat, LANES - 1, 1))
    up = jnp.where(y == 0, 0.0, pltpu.roll(flat, 1, 0))
    down = jnp.where(y == CELL - 1, 0.0, pltpu.roll(flat, count * CELL - 1, 0))
    return (0.5 * flat + 0.125 * (before + after + up + down)).reshape(cells.shape)


def update_kernel(
    n_row, n_col, sums_ref, own_ref, flip_ref, spread_ref, turned_ref, fresh_ref,
    table_s, fresh, rc, mid, rp, zb, rz,
    core_send, core_recv, p_send, p_recv, z_send, z_recv, send_sem, recv_sem,
):
    r, c, z, y, x, core, long, z_at, p_at = level_peers(n_row, n_col)
    p = x * 2 + y
    stored = own_ref.shape[0]
    share = stored // n_row
    low = lambda v: v.astype(jnp.bfloat16)
    high = lambda v: v.astype(jnp.float32)
    greet(gather_ids(n_row, n_col))
    order = [*range(1, long), 0]

    def make(src, dst, send, recv, at, peer):
        return pltpu.make_async_remote_copy(
            src_ref=src,
            dst_ref=dst,
            send_sem=send.at[at],
            recv_sem=recv.at[at],
            device_id=peer,
            device_id_type=MESH,
        )

    def chunk(side, t):
        return pl.ds((side * long + z_at(t)) * stored, stored)

    to_core = {}
    for t in order:
        src = sums_ref.at[chunk(1 - core, t)]
        to_core[t] = make(src, rc.at[t], core_send, core_recv, t, (x * 2 + 1 - core, c))
        to_core[t].start()
    to_p = {}
    for t in order:
        to_core[t].wait_recv()
        mid[t] = low(high(sums_ref[chunk(core, t)]) + high(rc[t]))
        for q in range(1, n_row):
            px, py = p_at(q)
            src = mid.at[t, pl.ds((px * 2 + py) * share, share)]
            at = t * n_row + q
            to_p[at] = make(src, rp.at[at], p_send, p_recv, at, (px * 2 + core, z * 2 + py))
            to_p[at].start()
    to_z = {}
    for t in order:
        total = high(mid[t, pl.ds(p * share, share)])
        for q in range(1, n_row):
            at = t * n_row + q
            to_p[at].wait_recv()
            total = total + high(rp[at])
        if t > 0:
            zb[t] = low(total)
            to_z[t] = make(zb.at[t], rz.at[t], z_send, z_recv, t, (r, z_at(t) * 2 + y))
            to_z[t].start()
    for t in range(1, long):
        to_z[t].wait_recv()
        total = total + high(rz[t])
    updated = own_ref[pl.ds(r * share, share)] - step_master * total
    value = low(smooth_packed(updated))
    fresh[...] = value
    table_s[pl.ds(c * stored + r * share, share)] = value

    def ready(at):
        turn_block(table_s, turned_ref, flip_ref, spread_ref, at, share)

    gather_levels(n_row, n_col, fresh, table_s, stored, send_sem, recv_sem, ready)
    fresh_ref[...] = high(table_s[pl.ds(c * stored, stored)])
    for copy in [*to_core.values(), *to_p.values(), *to_z.values()]:
        copy.wait_send()


def update_masters(sums, own, flip, spread, n_row, n_col):
    stored = own.shape[0]
    long = n_col // 2
    share = stored // n_row
    low = jnp.bfloat16
    cells = (CELL, LANES)
    sems = [pltpu.SemaphoreType.DMA((n,)) for n in (long, long, long * n_row, long * n_row, long, long)]
    return pl.pallas_call(
        functools.partial(update_kernel, n_row, n_col),
        in_specs=[VM, VM, VM, VM],
        out_specs=[VM, VM],
        out_shape=[
            jax.ShapeDtypeStruct((8 * sums.shape[0],) + cells, low),
            jax.ShapeDtypeStruct(own.shape, jnp.float32),
        ],
        scratch_shapes=[
            pltpu.VMEM(sums.shape, low),
            pltpu.VMEM((share,) + cells, low),
            pltpu.VMEM((long, stored) + cells, low),
            pltpu.VMEM((long, stored) + cells, low),
            pltpu.VMEM((long * n_row, share) + cells, low),
            pltpu.VMEM((long, share) + cells, low),
            pltpu.VMEM((long, share) + cells, low),
            *sems,
            *gather_sems(n_row, n_col),
        ],
        compiler_params=pltpu.CompilerParams(
            collective_id=2, has_side_effects=True, vmem_limit_bytes=32 * 1024 * 1024
        ),
        name="update_masters",
    )(sums, own, flip, spread)


def per_device(
    masters, inst_master, inst_orient, owner_map, tile_free, target, kernel_spectra, socs_weights
):
    stored = masters.shape[0] // 2
    total = owner_map.shape[0]
    consts = tables(TILE + 2 * HALO, kernel_spectra.shape[1], HALO, TILE)
    flip, spread = flips()
    own = masters.reshape(stored, 2, CELL, CELL).transpose(0, 2, 1, 3).reshape(stored, CELL, LANES)
    n_row = lax.axis_size("row")
    n_col = lax.axis_size("col")
    padded = front(
        inst_master, inst_orient, owner_map, own.astype(jnp.bfloat16), tile_free, flip, spread,
        n_row, n_col,
    )
    resist, new_free, sums = tile_steps(
        inst_master, inst_orient, owner_map, socs_weights, padded, target, tile_free,
        kernel_spectra, consts, flip, total, n_row, n_col,
    )
    turned, fresh = update_masters(sums, own, flip, spread, n_row, n_col)
    new_mask = image(inst_master, inst_orient, owner_map, turned, new_free)
    fresh = fresh.reshape(stored, CELL, 2, CELL).transpose(0, 2, 1, 3)
    return (resist, new_mask, fresh.reshape(masters.shape))


def solution(mesh):
    in_specs = (
        P("col", None),
        P("row", "col"),
        P("row", "col"),
        P(),
        P("row", "col"),
        P("row", "col"),
        P(),
        P(),
    )
    out_specs = (P("row", "col"), P("row", "col"), P("col", None))
    return jax.shard_map(
        per_device, mesh=mesh, in_specs=in_specs, out_specs=out_specs, check_vma=False
    )
```

```python
import functools
import math

import jax
import jax.numpy as jnp
import numpy as np
from jax import lax
from jax.experimental import pallas as pl
from jax.experimental.pallas import tpu as pltpu
from jax.sharding import PartitionSpec as P

TILE = 512
TPD = 2
HALO = 64
CELL = 64
LANES = 128
HALF = CELL // 2
STRIP = 16
GROUP = 4
SLAB = 256
VM = pl.BlockSpec(memory_space=pltpu.VMEM)
MESH = pl.DeviceIdType.MESH
GAIN_GRID = 1.9925
GAIN_SPREAD = 1.725625

step_free = 1.0
step_master = 0.05
resist_gain = 2.0
resist_level = 1.8


def dot(left, right):
    return jnp.dot(left, right, preferred_element_type=jnp.float32)


def bfloat(value):
    return jnp.asarray(np.ascontiguousarray(value).astype(jnp.bfloat16))


def tables(pad_side, band_side, halo, tile):
    freqs = np.arange(band_side, dtype=np.int64) - band_side // 2
    phases = (freqs[:, None] * np.arange(pad_side)[None, :]) % pad_side
    angles = phases.astype(np.float32) * np.float32(2.0 * math.pi / pad_side)
    cos = np.cos(angles)
    sin = np.sin(angles)
    cos_in = cos[:, halo : halo + tile]
    sin_in = sin[:, halo : halo + tile]
    cs_full = np.concatenate([cos, sin], 0)
    cs_lanes = np.pad(cs_full, ((0, 0), (LANES - halo, LANES - halo)))
    cs_in = np.concatenate([cos_in, sin_in], 0)
    grid = 2 * band_side
    turns = (freqs[:, None] * np.arange(grid)[None, :]) % grid
    cos_g = GAIN_GRID * np.cos(turns * (2.0 * math.pi / grid))
    sin_g = GAIN_GRID * np.sin(turns * (2.0 * math.pi / grid))
    cs_g = np.concatenate([cos_g, sin_g], 0)
    field = np.block([[cos_g, sin_g], [-sin_g, cos_g]])
    gaps = np.arange(halo, halo + tile)[:, None] / pad_side - np.arange(grid)[None, :] / grid
    waves = np.arange(1, band_side)
    spread = (1.0 + 2.0 * np.cos(2.0 * math.pi * gaps[:, :, None] * waves).sum(-1)) * (GAIN_SPREAD / grid)
    parts = (cs_full, cs_lanes.T, cs_g, cs_g.T, field, field.T, spread, spread.T, cs_in, cs_in.T)
    return [bfloat(p) for p in parts]


def flips():
    back = np.eye(CELL)[::-1]
    rows = np.kron(np.eye(4), back)
    same = np.eye(CELL)
    none = np.zeros((CELL, CELL))
    spread = [
        np.block([[m, m], [none, none]]) if e == 0 else np.block([[none, none], [m, m]])
        for m in (same, back)
        for e in range(2)
    ]
    return bfloat(rows), bfloat(np.concatenate(spread, 1))


def left_mask(rows):
    return lax.broadcasted_iota(jnp.int32, (rows, LANES), 1) < CELL


def pair_codes(inst_ref, orient_ref, owner_ref, a, b):
    s0 = owner_ref[inst_ref[a, b]]
    s1 = owner_ref[inst_ref[a, b + 1]]
    return s0, s1, orient_ref[a, b], orient_ref[a, b + 1]


def turn_block(table_ref, turned_ref, flip_ref, spread_ref, at, count):
    total = turned_ref.shape[0] // 4
    rows = count * CELL
    cells = table_ref[pl.ds(at, count)].reshape(rows, LANES)
    flipped = dot(flip_ref[:rows, :rows], cells).astype(jnp.bfloat16)
    both = dot(jnp.concatenate([cells, flipped], axis=0), spread_ref[...]).astype(jnp.bfloat16)
    for f in range(2):
        for c in range(2):
            for e in range(2):
                lanes = slice((2 * c + e) * LANES, (2 * c + e + 1) * LANES)
                for p in range(count):
                    start = f * rows + p * CELL
                    turned_ref[(2 * c + f) * total + 2 * (at + p) + e] = both[start : start + CELL, lanes]


def assemble_pair(turned_ref, codes):
    s0, s1, o0, o1 = codes
    total = turned_ref.shape[0] // 4
    one = turned_ref[o0 * total + s0].astype(jnp.float32)
    two = turned_ref[o1 * total + s1].astype(jnp.float32)
    return jnp.where(left_mask(CELL), one, two)


def image_kernel(inst_ref, orient_ref, owner_ref, turned_ref, free_ref, out_ref):
    steps = out_ref.shape[0] // CELL
    first = pl.program_id(0) * steps

    def step(a, carry):
        source = pl.ds(pl.multiple_of((first + a) * CELL, CELL), CELL)
        rows = pl.ds(pl.multiple_of(a * CELL, CELL), CELL)
        for pair in range(free_ref.shape[1] // LANES):
            codes = pair_codes(inst_ref, orient_ref, owner_ref, first + a, 2 * pair)
            cells = assemble_pair(turned_ref, codes)
            lanes = slice(pair * LANES, (pair + 1) * LANES)
            out_ref[rows, lanes] = jnp.tanh(cells + free_ref[source, lanes])
        return carry

    lax.fori_loop(0, steps, step, 0)


def whole_spec(array):
    zeros = (0,) * array.ndim
    return pl.BlockSpec(array.shape, lambda *_: zeros)


def image(inst, orient, owner, turned, free):
    height, width = free.shape
    strip = pl.BlockSpec((SLAB, width), lambda a, *_: (a, 0))
    return pl.pallas_call(
        image_kernel,
        grid_spec=pltpu.PrefetchScalarGridSpec(
            num_scalar_prefetch=3,
            grid=(height // SLAB,),
            in_specs=[VM, VM],
            out_specs=strip,
        ),
        out_shape=jax.ShapeDtypeStruct(free.shape, jnp.float32),
        compiler_params=pltpu.CompilerParams(vmem_limit_bytes=8 * 1024 * 1024),
        name="image",
    )(inst, orient, owner, turned, free)


def tile_kernel(
    n_row, n_col, inst_ref, orient_ref, owner_ref,
    padded_ref, target_ref, free_ref, kern_ref,
    cs_full_ref, cs_lanes_t_ref, cs_g_ref, cs_g_t_ref, field_ref, field_t_ref,
    spread_ref, spread_t_ref, cs_in_ref, cs_in_t_ref, flip_ref,
    resist_ref, new_free_ref, sums_ref,
    windows_s, kern_s, half_s, field_s, bhalf_s, level_s, turned_s, left_s, right_s,
    window_sem, kern_sem,
):
    i = pl.program_id(0)
    j = pl.program_id(1)
    band = kern_s.shape[2]
    kernels = kern_s.shape[1]
    tile = target_ref.shape[0]
    pad_side = cs_full_ref.shape[1]
    pad_lanes = cs_lanes_t_ref.shape[0]
    grid = 2 * band
    blocks = grid // STRIP
    low = lambda v: v.astype(jnp.bfloat16)

    wide = pl.num_programs(1)
    step = i * wide + j

    def fetch(n):
        rows = pl.ds(pl.multiple_of(n // wide * tile, tile), pad_side)
        lanes = pl.ds(pl.multiple_of(n % wide * tile, tile), pad_lanes)
        return pltpu.make_async_copy(
            padded_ref.at[rows, lanes], windows_s.at[n % 2], window_sem.at[n % 2]
        )

    load_kern = pltpu.make_async_copy(kern_ref, kern_s, kern_sem)

    @pl.when(step == 0)
    def _():
        fetch(0).start()
        load_kern.start()
        left_s[...] = jnp.zeros_like(left_s)
        right_s[...] = jnp.zeros_like(right_s)

    at_row = i * tile
    at_col = j * tile
    fetch(step).wait()

    @pl.when(step + 1 < pl.num_programs(0) * wide)
    def _():
        fetch(step + 1).start()

    here = step % 2
    window = windows_s[here]
    forw = low(dot(cs_full_ref[...], window))
    spec = dot(forw, cs_lanes_t_ref[...])
    spec_re = spec[:band, :band] + spec[band:, band:]
    spec_im = spec[band:, :band] - spec[:band, band:]

    @pl.when(step == 0)
    def _():
        load_kern.wait()

    for k in range(kernels):
        amp_re = low(kern_s[0, k] * spec_re - kern_s[1, k] * spec_im)
        amp_im = low(kern_s[0, k] * spec_im + kern_s[1, k] * spec_re)
        upper = jnp.concatenate([amp_re, amp_im], axis=1)
        lower = jnp.concatenate([-amp_im, amp_re], axis=1)
        half = low(dot(cs_g_t_ref[...], jnp.concatenate([upper, lower], axis=0)))
        half_s[:, k] = half.reshape(blocks, STRIP, grid)
    for b in range(0, blocks, GROUP):
        lines = half_s[b : b + GROUP].reshape(GROUP * kernels * STRIP, grid)
        field = dot(lines, field_ref[...])
        re = field[:, :grid]
        im = field[:, grid:]
        power = (re * re + im * im).reshape(GROUP, kernels, STRIP, grid)
        level_s[b : b + GROUP] = jnp.sum(power, axis=1)
        field_s[b : b + GROUP] = low(field).reshape(GROUP, kernels, STRIP, 2 * grid)
    level = level_s[...].reshape(grid, grid)
    mean = jnp.sum(jnp.sum(level, axis=0, keepdims=True), axis=1, keepdims=True) / (grid * grid)
    lines = low(dot(spread_ref[...], low(level - mean)))
    above = (mean - resist_level) * (0.5 * resist_gain)
    swing = jnp.tanh(dot(lines, spread_t_ref[...]) * (0.5 * resist_gain / GAIN_SPREAD**2) + above)
    resist = 0.5 * swing + 0.5
    resist_ref[...] = resist
    top = resist_gain / GAIN_SPREAD**2
    slopes = (resist - target_ref[...]) * (top - top * (swing * swing))
    lines = low(dot(spread_t_ref[...], low(slopes)))
    pulls = low(dot(lines, spread_ref[...])).reshape(blocks, 1, STRIP, grid)
    for b in range(0, blocks, GROUP):
        pull = jnp.concatenate([pulls[b : b + GROUP]] * 2, axis=3)
        back = field_s[b : b + GROUP] * pull
        bhalf = low(dot(back.reshape(GROUP * kernels * STRIP, 2 * grid), field_t_ref[...]))
        bhalf = bhalf.reshape(GROUP, kernels, STRIP, grid)
        for g in range(GROUP):
            bhalf_s[:, b + g] = bhalf[g]
    bspec_re = jnp.zeros((band, band), jnp.float32)
    bspec_im = jnp.zeros((band, band), jnp.float32)
    for k in range(kernels):
        bamp = dot(cs_g_ref[...], bhalf_s[k].reshape(grid, grid))
        bamp_re = bamp[:band, :band] + bamp[band:, band:]
        bamp_im = bamp[:band, band:] - bamp[band:, :band]
        bspec_re += kern_s[0, k] * bamp_re + kern_s[1, k] * bamp_im
        bspec_im += kern_s[0, k] * bamp_im - kern_s[1, k] * bamp_re
    upper = jnp.concatenate([low(bspec_re), low(-bspec_im)], axis=1)
    lower = jnp.concatenate([low(bspec_im), low(bspec_re)], axis=1)
    bforw = low(dot(jnp.concatenate([upper, lower], axis=0), cs_in_ref[...]))
    gradient = dot(cs_in_t_ref[...], bforw)
    shading = windows_s[here, HALO : HALO + tile, LANES : LANES + tile].astype(jnp.float32)
    grad_param = gradient * (1.0 - shading * shading)
    new_free_ref[
        pl.ds(pl.multiple_of(at_row, tile), tile), pl.ds(pl.multiple_of(at_col, tile), tile)
    ] = free_ref[...] - step_free * grad_param
    turned_s[0] = grad_param
    plain = low(grad_param)
    group = flip_ref.shape[0]
    for at in range(0, tile, group):
        part = slice(at, at + group)
        across = dot(plain[:, part], flip_ref[...])
        turned_s[2, :, part] = across
        for f, source in ((1, plain[:, part]), (3, low(across))):
            for up in range(0, tile, group):
                turned_s[f, up : up + group, part] = dot(flip_ref[...], source[up : up + group])
    cells = tile // CELL
    left = left_mask(CELL)

    def cells_step(a, carry):
        rows = pl.ds(pl.multiple_of(a * CELL, CELL), CELL)
        for pair in range(cells // 2):
            s0, s1, o0, o1 = pair_codes(
                inst_ref, orient_ref, owner_ref, i * cells + a, j * cells + 2 * pair
            )
            lanes = slice(pair * LANES, (pair + 1) * LANES)
            left_s[s0] += turned_s[o0, rows, lanes]
            right_s[s1] += turned_s[o1, rows, lanes]
        return carry

    lax.fori_loop(0, cells, cells_step, 0)

    @pl.when((i == pl.num_programs(0) - 1) & (j == pl.num_programs(1) - 1))
    def _():
        stored = sums_ref.shape[0] // n_col
        share = stored // n_row

        def pack(p, carry):
            one = left_s[2 * p] + pltpu.roll(right_s[2 * p], CELL, 1)
            two = pltpu.roll(left_s[2 * p + 1], CELL, 1) + right_s[2 * p + 1]
            col = p // stored
            row = p % stored // share
            side = row % 2 * (n_col // 2) + col // 2
            spot = (side * n_row + row // 2 * 2 + col % 2) * share + p % share
            sums_ref[spot] = low(jnp.where(left, one, two))
            return carry

        lax.fori_loop(0, sums_ref.shape[0], pack, 0)


def tile_steps(inst, orient, owner, padded, target, free, kern, consts, flip, masters, n_row, n_col):
    height, width = target.shape
    kernels, band = kern.shape[1:3]
    grid = 2 * band
    blocks = grid // STRIP
    tile_spec = pl.BlockSpec((TILE, TILE), lambda i, j, *_: (i, j))
    hbm = pl.BlockSpec(memory_space=pltpu.HBM)
    sums_shape = (masters // 2, CELL, LANES)
    return pl.pallas_call(
        functools.partial(tile_kernel, n_row, n_col),
        grid_spec=pltpu.PrefetchScalarGridSpec(
            num_scalar_prefetch=3,
            grid=(height // TILE, width // TILE),
            in_specs=[hbm, tile_spec, tile_spec, hbm, *[VM] * len(consts), VM],
            out_specs=[tile_spec, VM, VM],
            scratch_shapes=[
                pltpu.VMEM((2, TILE + 2 * HALO, TILE + 2 * LANES), jnp.bfloat16),
                pltpu.VMEM(kern.shape, jnp.float32),
                pltpu.VMEM((blocks, kernels, STRIP, grid), jnp.bfloat16),
                pltpu.VMEM((blocks, kernels, STRIP, 2 * grid), jnp.bfloat16),
                pltpu.VMEM((kernels, blocks, STRIP, grid), jnp.bfloat16),
                pltpu.VMEM((blocks, STRIP, grid), jnp.float32),
                pltpu.VMEM((4, TILE, TILE), jnp.float32),
                pltpu.VMEM((masters, CELL, LANES), jnp.float32),
                pltpu.VMEM((masters, CELL, LANES), jnp.float32),
                pltpu.SemaphoreType.DMA((2,)),
                pltpu.SemaphoreType.DMA,
            ],
        ),
        out_shape=[
            jax.ShapeDtypeStruct(target.shape, jnp.float32),
            jax.ShapeDtypeStruct(target.shape, jnp.float32),
            jax.ShapeDtypeStruct(sums_shape, jnp.bfloat16),
        ],
        compiler_params=pltpu.CompilerParams(vmem_limit_bytes=36 * 1024 * 1024),
        name="tile_steps",
    )(inst, orient, owner, padded, target, free, kern, *consts, flip)


def greet(peers):
    barrier = pltpu.get_barrier_semaphore()
    for peer in peers:
        pl.semaphore_signal(barrier, inc=1, device_id=peer, device_id_type=MESH)
    pl.semaphore_wait(barrier, len(peers))


def level_peers(n_row, n_col):
    r = lax.axis_index("row")
    c = lax.axis_index("col")
    long = n_col // 2
    z, y = lax.div(c, 2), lax.rem(c, 2)
    x, core = lax.div(r, 2), lax.rem(r, 2)
    p = x * 2 + y

    def z_at(t):
        return lax.rem(z + t + long, long)

    def p_at(t):
        q = lax.rem(p + t + n_row, n_row)
        return lax.div(q, 2), lax.rem(q, 2)

    return r, c, z, y, x, core, long, z_at, p_at


def gather_ids(n_row, n_col):
    r, c, z, y, x, core, long, z_at, p_at = level_peers(n_row, n_col)
    ids = [(r, z_at(t) * 2 + y) for t in range(1, long)]
    for t in range(1, n_row):
        px, py = p_at(t)
        ids.append((px * 2 + core, z * 2 + py))
    return ids + [(x * 2 + 1 - core, c)]


def gather_levels(n_row, n_col, own, table_ref, stored, send_sem, recv_sem, started, ready):
    r, c, z, y, x, core, long, z_at, p_at = level_peers(n_row, n_col)
    share = stored // n_row
    partner = (x * 2 + 1 - core, c)

    def first_row(row, col):
        return col * stored + row * share

    def make(src, at, level, slot, peer):
        return pltpu.make_async_remote_copy(
            src_ref=src,
            dst_ref=table_ref.at[pl.ds(at, share)],
            send_sem=send_sem.at[level, slot],
            recv_sem=recv_sem.at[level, slot],
            device_id=peer,
            device_id_type=MESH,
        )

    def here(at):
        return table_ref.at[pl.ds(at, share)]

    mine = first_row(r, c)
    first = [make(own, mine, 0, t, (r, z_at(t) * 2 + y)) for t in range(1, long)]
    for copy in first:
        copy.start()
    started()
    second = []
    third = []
    for t in range(long):
        if t > 0:
            first[t - 1].wait_recv()
        at = first_row(r, z_at(-t) * 2 + y)
        src = own if t == 0 else here(at)
        for q in range(1, n_row):
            px, py = p_at(q)
            copy = make(src, at, 1, t * n_row + q, (px * 2 + core, z * 2 + py))
            copy.start()
            second.append(copy)
        copy = make(src, at, 2, t * n_row, partner)
        copy.start()
        third.append(copy)
    for t in range(long):
        ready(first_row(r, z_at(-t) * 2 + y))

    def across(n, carry):
        t = n // (n_row - 1)
        q = n % (n_row - 1) + 1
        slot = t * n_row + q
        px, py = p_at(-q)
        at = first_row(px * 2 + core, z_at(-t) * 2 + py)
        make(here(at), at, 1, slot, partner).wait_recv()
        make(here(at), at, 2, slot, partner).start()
        ready(at)
        return carry

    def beside(n, carry):
        t = n // n_row
        q = n % n_row
        px, py = p_at(-q)
        at = first_row(px * 2 + 1 - core, z_at(-t) * 2 + py)
        make(here(at), at, 2, n, partner).wait_recv()
        ready(at)
        return carry

    def sent(n, carry):
        make(here(mine), mine, 2, n, partner).wait_send()
        return carry

    lax.fori_loop(0, long * (n_row - 1), across, 0)
    lax.fori_loop(0, long * n_row, beside, 0)
    for copy in first + second:
        copy.wait_send()
    lax.fori_loop(0, long * n_row, sent, 0)


def gather_sems(n_row, n_col):
    shape = (3, n_row * n_col // 2)
    return [pltpu.SemaphoreType.DMA(shape), pltpu.SemaphoreType.DMA(shape)]


def front_kernel(
    n_row, n_col, weights_ref, codes_refs, own_ref, free_ref, flip_hbm, spread_hbm, spectra_ref,
    out_hbm, kern_hbm,
    out_ref, kern_ref, codes_s, table_s, turned_s, free_s, flip_ref, spread_ref, edge_l, edge_r, from_l, from_r,
    load_sem, kern_sem, save_sem, send_sem, recv_sem, halo_send, halo_recv,
):
    r = lax.axis_index("row")
    c = lax.axis_index("col")
    height, width = free_s.shape
    packed = height // 2
    stored = own_ref.shape[0]
    share = stored // n_row
    inst_ref, orient_ref, owner_ref = codes_s
    band, kernels = kern_ref.shape[2], kern_ref.shape[1]
    pad_side = TILE + 2 * HALO
    loads = [(flip_hbm, flip_ref), (spread_hbm, spread_ref), *zip(codes_refs, codes_s), (free_ref, free_s)]
    loads = [pltpu.make_async_copy(src, dst, load_sem.at[n]) for n, (src, dst) in enumerate(loads)]
    for part in range(2):
        for k in range(kernels):
            src = spectra_ref.at[part, :, k, :]
            loads.append(pltpu.make_async_copy(src, kern_ref.at[part, k], kern_sem.at[part, k]))
    for load in loads:
        load.start()
    moves = [(0, 1), (0, -1), (1, 0), (-1, 0), (1, 1), (1, -1), (-1, 1), (-1, -1)]
    ids = [(lax.rem(r + n_row + dr, n_row), lax.rem(c + n_col + dc, n_col)) for dr, dc in moves]
    greet(gather_ids(n_row, n_col) + ids)
    own = own_ref.at[pl.ds(r * share, share)]
    table_s[pl.ds(c * stored + r * share, share)] = own_ref[pl.ds(r * share, share)]

    def started():
        for load in loads:
            load.wait()
        for k in range(kernels):
            weight = jnp.full((band, LANES), weights_ref[k], jnp.float32)
            scale = jnp.sqrt(weight) / (pad_side * band * GAIN_GRID**2)
            for part in range(2):
                kern_ref[part, k] = kern_ref[part, k] * scale

    def save(n, *at):
        return pltpu.make_async_copy(out_ref.at[at], out_hbm.at[at], save_sem.at[n])

    save_kern = pltpu.make_async_copy(kern_ref, kern_hbm, save_sem.at[5])

    def ready(at):
        turn_block(table_s, turned_s, flip_ref, spread_ref, at, share)

    gather_levels(n_row, n_col, own, table_s, stored, send_sem, recv_sem, started, ready)

    pairs = width // LANES
    strips = height // CELL
    cast = lambda v: v.astype(jnp.bfloat16)
    left = left_mask(HALF)

    def draw(a, pair):
        codes = pair_codes(inst_ref, orient_ref, owner_ref, a, 2 * pair)
        cells = assemble_pair(turned_s, codes)
        rows = pl.ds(pl.multiple_of(a * CELL, CELL), CELL)
        value = jnp.tanh(cells + free_s[rows, pair * LANES : (pair + 1) * LANES])
        rows = pl.ds(pl.multiple_of(HALO + a * CELL, CELL), CELL)
        out_ref[rows, (pair + 1) * LANES : (pair + 2) * LANES] = cast(value)
        return value

    def outer(n, carry):
        for pair in range(1, pairs - 1):
            draw(n * (strips - 1), pair)
        return carry

    def sides(a, carry):
        rows = pl.ds(pl.multiple_of(a * HALF, HALF), HALF)
        value = draw(a, 0)
        edge_l[rows] = cast(jnp.where(left, value[:HALF], pltpu.roll(value[HALF:], CELL, 1)))
        value = draw(a, pairs - 1)
        edge_r[rows] = cast(jnp.where(left, pltpu.roll(value[:HALF], CELL, 1), value[HALF:]))
        return carry

    def inner(a, carry):
        for pair in range(1, pairs - 1):
            draw(a, pair)
        return carry

    lax.fori_loop(0, 2, outer, 0)
    lax.fori_loop(0, strips, sides, 0)
    lax.fori_loop(1, 3, inner, 0)

    middle = slice(LANES, LANES + width)
    row_parts = {
        -1: (slice(HALO, 2 * HALO), slice(HALO + height, 2 * HALO + height)),
        1: (slice(height, HALO + height), slice(0, HALO)),
    }
    edge_parts = {
        -1: (slice(0, HALF), slice(HALF + packed, 2 * HALF + packed)),
        0: (slice(0, packed), slice(HALF, HALF + packed)),
        1: (slice(packed - HALF, packed), slice(0, HALF)),
    }

    def inside(dr, dc):
        return (r + dr >= 0) & (r + dr < n_row) & (c + dc >= 0) & (c + dc < n_col)

    work = []
    for at, (dr, dc) in enumerate(moves):
        if dc == 0:
            src, dst = row_parts[dr]
            src, dst = out_ref.at[src, middle], out_ref.at[dst, middle]
        else:
            src, dst = edge_parts[dr]
            src = (edge_r if dc == 1 else edge_l).at[src]
            dst = (from_l if dc == 1 else from_r).at[dst]
        copy = pltpu.make_async_remote_copy(
            src_ref=src,
            dst_ref=dst,
            send_sem=halo_send.at[at],
            recv_sem=halo_recv.at[at],
            device_id=ids[at],
            device_id_type=MESH,
        )
        work.append((copy, dst, inside(dr, dc), inside(-dr, -dc)))
    for copy, dst, sends, gets in work:
        pl.when(sends)(copy.start)
    lax.fori_loop(3, strips - 1, inner, 0)
    lines = slice(HALO, HALO + height)
    saves = [save(0, lines, middle), save_kern]
    for copy in saves:
        copy.start()
    for copy, dst, sends, gets in work:

        @pl.when(jnp.logical_not(gets))
        def _():
            dst[...] = jnp.zeros(dst.shape, dst.dtype)

    for copy, dst, sends, gets in work:
        pl.when(gets)(copy.wait_recv)

    def unpack(a, carry):
        rows = pl.ds(pl.multiple_of(a * HALF, HALF), HALF)
        upper = pl.ds(pl.multiple_of(a * CELL, CELL), HALF)
        lower = pl.ds(pl.multiple_of(a * CELL + HALF, HALF), HALF)
        one = from_l[rows].astype(jnp.float32)
        two = from_r[rows].astype(jnp.float32)
        last = slice(LANES + width, 2 * LANES + width)
        out_ref[upper, :LANES] = cast(jnp.where(left, 0.0, pltpu.roll(one, CELL, 1)))
        out_ref[lower, :LANES] = cast(jnp.where(left, 0.0, one))
        out_ref[upper, last] = cast(jnp.where(left, two, 0.0))
        out_ref[lower, last] = cast(jnp.where(left, pltpu.roll(two, CELL, 1), 0.0))
        return carry

    lax.fori_loop(0, (height + 2 * HALO) // CELL, unpack, 0)
    last = [
        save(1, slice(0, HALO)),
        save(2, slice(HALO + height, 2 * HALO + height)),
        save(3, lines, slice(0, LANES)),
        save(4, lines, slice(LANES + width, 2 * LANES + width)),
    ]
    for copy in last:
        copy.start()
    for copy, dst, sends, gets in work:
        pl.when(sends)(copy.wait_send)
    for copy in saves + last:
        copy.wait()


def front(codes, weights, own, free, flip, spread, spectra, n_row, n_col):
    height, width = free.shape
    smem = pl.BlockSpec(memory_space=pltpu.SMEM)
    hbm = pl.BlockSpec(memory_space=pltpu.HBM)
    low = jnp.bfloat16
    pairs = n_col * own.shape[0]
    band, kernels = spectra.shape[1:3]
    return pl.pallas_call(
        functools.partial(front_kernel, n_row, n_col),
        in_specs=[smem, [hbm] * 3, VM, hbm, hbm, hbm, hbm],
        out_specs=[hbm, hbm],
        out_shape=[
            jax.ShapeDtypeStruct((height + 2 * HALO, width + 2 * LANES), low),
            jax.ShapeDtypeStruct((2, kernels, band, band), jnp.float32),
        ],
        scratch_shapes=[
            pltpu.VMEM((height + 2 * HALO, width + 2 * LANES), low),
            pltpu.VMEM((2, kernels, band, band), jnp.float32),
            [pltpu.SMEM(v.shape, v.dtype) for v in codes],
            pltpu.VMEM((pairs, CELL, LANES), low),
            pltpu.VMEM((8 * pairs, CELL, LANES), low),
            pltpu.VMEM((height, width), jnp.float32),
            pltpu.VMEM(flip.shape, low),
            pltpu.VMEM(spread.shape, low),
            pltpu.VMEM((height // 2, LANES), low),
            pltpu.VMEM((height // 2, LANES), low),
            pltpu.VMEM((height // 2 + 2 * HALF, LANES), low),
            pltpu.VMEM((height // 2 + 2 * HALF, LANES), low),
            pltpu.SemaphoreType.DMA((6,)),
            pltpu.SemaphoreType.DMA((2, kernels)),
            pltpu.SemaphoreType.DMA((6,)),
            *gather_sems(n_row, n_col),
            pltpu.SemaphoreType.DMA((8,)),
            pltpu.SemaphoreType.DMA((8,)),
        ],
        compiler_params=pltpu.CompilerParams(
            collective_id=0, has_side_effects=True, vmem_limit_bytes=56 * 1024 * 1024
        ),
        name="front",
    )(weights, codes, own, free, flip, spread, spectra)


def smooth_packed(cells):
    count = cells.shape[0]
    flat = cells.reshape(count * CELL, LANES)
    x = lax.broadcasted_iota(jnp.int32, flat.shape, 1) % CELL
    y = lax.broadcasted_iota(jnp.int32, flat.shape, 0) % CELL
    before = jnp.where(x == 0, 0.0, pltpu.roll(flat, 1, 1))
    after = jnp.where(x == CELL - 1, 0.0, pltpu.roll(flat, LANES - 1, 1))
    up = jnp.where(y == 0, 0.0, pltpu.roll(flat, 1, 0))
    down = jnp.where(y == CELL - 1, 0.0, pltpu.roll(flat, count * CELL - 1, 0))
    return (0.5 * flat + 0.125 * (before + after + up + down)).reshape(cells.shape)


def update_kernel(
    n_row, n_col, sums_ref, own_ref, flip_ref, spread_ref, turned_ref, fresh_ref,
    table_s, fresh, rc, mid, rp, zb, rz,
    core_send, core_recv, p_send, p_recv, z_send, z_recv, send_sem, recv_sem,
):
    r, c, z, y, x, core, long, z_at, p_at = level_peers(n_row, n_col)
    p = x * 2 + y
    stored = own_ref.shape[0]
    share = stored // n_row
    low = lambda v: v.astype(jnp.bfloat16)
    high = lambda v: v.astype(jnp.float32)
    greet(gather_ids(n_row, n_col))
    order = [*range(1, long), 0]

    def make(src, dst, send, recv, at, peer):
        return pltpu.make_async_remote_copy(
            src_ref=src,
            dst_ref=dst,
            send_sem=send.at[at],
            recv_sem=recv.at[at],
            device_id=peer,
            device_id_type=MESH,
        )

    def chunk(side, t):
        return pl.ds((side * long + z_at(t)) * stored, stored)

    to_core = {}
    for t in order:
        src = sums_ref.at[chunk(1 - core, t)]
        to_core[t] = make(src, rc.at[t], core_send, core_recv, t, (x * 2 + 1 - core, c))
        to_core[t].start()
    to_p = {}
    for t in order:
        to_core[t].wait_recv()
        mid[t] = low(high(sums_ref[chunk(core, t)]) + high(rc[t]))
        for q in range(1, n_row):
            px, py = p_at(q)
            src = mid.at[t, pl.ds((px * 2 + py) * share, share)]
            at = t * n_row + q
            to_p[at] = make(src, rp.at[at], p_send, p_recv, at, (px * 2 + core, z * 2 + py))
            to_p[at].start()
    to_z = {}
    for t in order:
        total = high(mid[t, pl.ds(p * share, share)])
        for q in range(1, n_row):
            at = t * n_row + q
            to_p[at].wait_recv()
            total = total + high(rp[at])
        if t > 0:
            zb[t] = low(total)
            to_z[t] = make(zb.at[t], rz.at[t], z_send, z_recv, t, (r, z_at(t) * 2 + y))
            to_z[t].start()
    for t in range(1, long):
        to_z[t].wait_recv()
        total = total + high(rz[t])
    updated = own_ref[pl.ds(r * share, share)] - step_master * total
    value = low(smooth_packed(updated))
    fresh[...] = value
    table_s[pl.ds(c * stored + r * share, share)] = value

    def ready(at):
        turn_block(table_s, turned_ref, flip_ref, spread_ref, at, share)

    gather_levels(n_row, n_col, fresh, table_s, stored, send_sem, recv_sem, lambda: None, ready)
    fresh_ref[...] = high(table_s[pl.ds(c * stored, stored)])
    for copy in [*to_core.values(), *to_p.values(), *to_z.values()]:
        copy.wait_send()


def update_masters(sums, own, flip, spread, n_row, n_col):
    stored = own.shape[0]
    long = n_col // 2
    share = stored // n_row
    low = jnp.bfloat16
    cells = (CELL, LANES)
    sems = [pltpu.SemaphoreType.DMA((n,)) for n in (long, long, long * n_row, long * n_row, long, long)]
    return pl.pallas_call(
        functools.partial(update_kernel, n_row, n_col),
        in_specs=[VM, VM, VM, VM],
        out_specs=[VM, VM],
        out_shape=[
            jax.ShapeDtypeStruct((8 * sums.shape[0],) + cells, low),
            jax.ShapeDtypeStruct(own.shape, jnp.float32),
        ],
        scratch_shapes=[
            pltpu.VMEM(sums.shape, low),
            pltpu.VMEM((share,) + cells, low),
            pltpu.VMEM((long, stored) + cells, low),
            pltpu.VMEM((long, stored) + cells, low),
            pltpu.VMEM((long * n_row, share) + cells, low),
            pltpu.VMEM((long, share) + cells, low),
            pltpu.VMEM((long, share) + cells, low),
            *sems,
            *gather_sems(n_row, n_col),
        ],
        compiler_params=pltpu.CompilerParams(
            collective_id=2, has_side_effects=True, vmem_limit_bytes=16 * 1024 * 1024
        ),
        name="update_masters",
    )(sums, own, flip, spread)


def per_device(
    masters, inst_master, inst_orient, owner_map, tile_free, target, kernel_spectra, socs_weights
):
    stored = masters.shape[0] // 2
    total = owner_map.shape[0]
    consts = tables(TILE + 2 * HALO, kernel_spectra.shape[1], HALO, TILE)
    flip, spread = flips()
    own = masters.reshape(stored, 2, CELL, CELL).transpose(0, 2, 1, 3).reshape(stored, CELL, LANES)
    n_row = lax.axis_size("row")
    n_col = lax.axis_size("col")
    codes = [inst_master, inst_orient, owner_map]
    padded, kern = front(
        codes, socs_weights, own.astype(jnp.bfloat16), tile_free, flip, spread, kernel_spectra,
        n_row, n_col,
    )
    resist, new_free, sums = tile_steps(
        *codes, padded, target, tile_free, kern, consts, flip, total, n_row, n_col
    )
    turned, fresh = update_masters(sums, own, flip, spread, n_row, n_col)
    new_mask = image(inst_master, inst_orient, owner_map, turned, new_free)
    fresh = fresh.reshape(stored, CELL, 2, CELL).transpose(0, 2, 1, 3)
    return (resist, new_mask, fresh.reshape(masters.shape))


def solution(mesh):
    in_specs = (
        P("col", None),
        P("row", "col"),
        P("row", "col"),
        P(),
        P("row", "col"),
        P("row", "col"),
        P(),
        P(),
    )
    out_specs = (P("row", "col"), P("row", "col"), P("col", None))
    return jax.shard_map(
        per_device, mesh=mesh, in_specs=in_specs, out_specs=out_specs, check_vma=False
    )
```

```python
import functools
import math

import jax
import jax.numpy as jnp
import numpy as np
from jax import lax
from jax.experimental import pallas as pl
from jax.experimental.pallas import tpu as pltpu
from jax.sharding import PartitionSpec as P

TILE = 512
TPD = 2
HALO = 64
CELL = 64
LANES = 128
HALF = CELL // 2
STRIP = 16
GROUP = 4
SLAB = 256
VM = pl.BlockSpec(memory_space=pltpu.VMEM)
MESH = pl.DeviceIdType.MESH
FRONT_MIB = 56
TILE_MIB = 50
UPDATE_MIB = 16
IMAGE_MIB = 8
GAIN_GRID = 1.9925
GAIN_SPREAD = 1.725625

step_free = 1.0
step_master = 0.05
resist_gain = 2.0
resist_level = 1.8


def dot(left, right):
    return jnp.dot(left, right, preferred_element_type=jnp.float32)


def bfloat(value):
    return jnp.asarray(np.ascontiguousarray(value).astype(jnp.bfloat16))


def tables(pad_side, band_side, halo, tile):
    freqs = np.arange(band_side, dtype=np.int64) - band_side // 2
    phases = (freqs[:, None] * np.arange(pad_side)[None, :]) % pad_side
    angles = phases.astype(np.float32) * np.float32(2.0 * math.pi / pad_side)
    cos = np.cos(angles)
    sin = np.sin(angles)
    cos_in = cos[:, halo : halo + tile]
    sin_in = sin[:, halo : halo + tile]
    cs_full = np.concatenate([cos, sin], 0)
    cs_lanes = np.pad(cs_full, ((0, 0), (LANES - halo, LANES - halo)))
    cs_in = np.concatenate([cos_in, sin_in], 0)
    grid = 2 * band_side
    turns = (freqs[:, None] * np.arange(grid)[None, :]) % grid
    cos_g = GAIN_GRID * np.cos(turns * (2.0 * math.pi / grid))
    sin_g = GAIN_GRID * np.sin(turns * (2.0 * math.pi / grid))
    cs_g = np.concatenate([cos_g, sin_g], 0)
    field = np.block([[cos_g, sin_g], [-sin_g, cos_g]])
    gaps = np.arange(halo, halo + tile)[:, None] / pad_side - np.arange(grid)[None, :] / grid
    waves = np.arange(1, band_side)
    spread = (1.0 + 2.0 * np.cos(2.0 * math.pi * gaps[:, :, None] * waves).sum(-1)) * (GAIN_SPREAD / grid)
    parts = (cs_full, cs_lanes.T, cs_g, cs_g.T, field, field.T, spread, spread.T, cs_in, cs_in.T)
    return [bfloat(p) for p in parts]


def flips():
    back = np.eye(CELL)[::-1]
    rows = np.kron(np.eye(4), back)
    same = np.eye(CELL)
    none = np.zeros((CELL, CELL))
    spread = [
        np.block([[m, m], [none, none]]) if e == 0 else np.block([[none, none], [m, m]])
        for m in (same, back)
        for e in range(2)
    ]
    return bfloat(rows), bfloat(np.concatenate(spread, 1))


def left_mask(rows):
    return lax.broadcasted_iota(jnp.int32, (rows, LANES), 1) < CELL


def pair_codes(inst_ref, orient_ref, owner_ref, a, b):
    s0 = owner_ref[inst_ref[a, b]]
    s1 = owner_ref[inst_ref[a, b + 1]]
    return s0, s1, orient_ref[a, b], orient_ref[a, b + 1]


def turn_blocks(table_ref, turned_ref, flip_ref, spread_ref, spots, count):
    total = turned_ref.shape[0] // 4
    rows = count * CELL
    most = flip_ref.shape[0] // rows
    for first in range(0, len(spots), most):
        some = spots[first : first + most]
        cells = [table_ref[pl.ds(at, count)].reshape(rows, LANES) for at in some]
        cells = jnp.concatenate(cells, axis=0) if len(some) > 1 else cells[0]
        full = len(some) * rows
        flipped = dot(flip_ref[:full, :full], cells).astype(jnp.bfloat16)
        both = dot(jnp.concatenate([cells, flipped], axis=0), spread_ref[...]).astype(jnp.bfloat16)
        for f in range(2):
            for c in range(2):
                for e in range(2):
                    lanes = slice((2 * c + e) * LANES, (2 * c + e + 1) * LANES)
                    for n, at in enumerate(some):
                        for p in range(count):
                            start = f * full + n * rows + p * CELL
                            spot = (2 * c + f) * total + 2 * (at + p) + e
                            turned_ref[spot] = both[start : start + CELL, lanes]


def assemble_pair(turned_ref, codes):
    s0, s1, o0, o1 = codes
    total = turned_ref.shape[0] // 4
    one = turned_ref[o0 * total + s0].astype(jnp.float32)
    two = turned_ref[o1 * total + s1].astype(jnp.float32)
    return jnp.where(left_mask(CELL), one, two)


def image_kernel(inst_ref, orient_ref, owner_ref, turned_ref, free_ref, out_ref):
    steps = out_ref.shape[0] // CELL
    first = pl.program_id(0) * steps

    def step(a, carry):
        rows = pl.ds(pl.multiple_of(a * CELL, CELL), CELL)
        for pair in range(free_ref.shape[1] // LANES):
            codes = pair_codes(inst_ref, orient_ref, owner_ref, first + a, 2 * pair)
            cells = assemble_pair(turned_ref, codes)
            lanes = slice(pair * LANES, (pair + 1) * LANES)
            out_ref[rows, lanes] = jnp.tanh(cells + free_ref[rows, lanes])
        return carry

    lax.fori_loop(0, steps, step, 0)


def whole_spec(array):
    zeros = (0,) * array.ndim
    return pl.BlockSpec(array.shape, lambda *_: zeros)


def image(inst, orient, owner, turned, free):
    height, width = free.shape
    strip = pl.BlockSpec((SLAB, width), lambda a, *_: (a, 0))
    return pl.pallas_call(
        image_kernel,
        grid_spec=pltpu.PrefetchScalarGridSpec(
            num_scalar_prefetch=3,
            grid=(height // SLAB,),
            in_specs=[VM, strip],
            out_specs=strip,
        ),
        out_shape=jax.ShapeDtypeStruct(free.shape, jnp.float32),
        compiler_params=pltpu.CompilerParams(vmem_limit_bytes=IMAGE_MIB * 1024 * 1024),
        input_output_aliases={4: 0},
        name="image",
    )(inst, orient, owner, turned, free)


def tile_kernel(
    n_row, n_col, inst_ref, orient_ref, owner_ref, weights_ref,
    padded_ref, target_ref, free_ref, spectra_ref,
    cs_full_ref, cs_lanes_t_ref, cs_g_ref, cs_g_t_ref, field_ref, field_t_ref,
    spread_ref, spread_t_ref, cs_in_ref, cs_in_t_ref, flip_ref,
    resist_ref, new_free_ref, sums_ref,
    windows_s, kern_s, half_s, field_s, bhalf_s, level_s, turned_s, left_s, right_s,
    window_sem, kern_sem,
):
    i = pl.program_id(0)
    j = pl.program_id(1)
    band = kern_s.shape[2]
    kernels = kern_s.shape[1]
    tile = target_ref.shape[0]
    pad_side = cs_full_ref.shape[1]
    pad_lanes = cs_lanes_t_ref.shape[0]
    grid = 2 * band
    blocks = grid // STRIP
    low = lambda v: v.astype(jnp.bfloat16)

    wide = pl.num_programs(1)
    step = i * wide + j

    def fetch(n):
        rows = pl.ds(pl.multiple_of(n // wide * tile, tile), pad_side)
        lanes = pl.ds(pl.multiple_of(n % wide * tile, tile), pad_lanes)
        return pltpu.make_async_copy(
            padded_ref.at[rows, lanes], windows_s.at[n % 2], window_sem.at[n % 2]
        )

    def load_kern(part, k):
        return pltpu.make_async_copy(
            spectra_ref.at[part, :, k, :], kern_s.at[part, k], kern_sem.at[part, k]
        )

    @pl.when(step == 0)
    def _():
        fetch(0).start()
        for k in range(kernels):
            load_kern(0, k).start()
            load_kern(1, k).start()
        left_s[...] = jnp.zeros_like(left_s)
        right_s[...] = jnp.zeros_like(right_s)

    fetch(step).wait()

    @pl.when(step + 1 < pl.num_programs(0) * wide)
    def _():
        fetch(step + 1).start()

    here = step % 2
    window = windows_s[here]
    forw = low(dot(cs_full_ref[...], window))
    spec = dot(forw, cs_lanes_t_ref[...])
    spec_re = spec[:band, :band] + spec[band:, band:]
    spec_im = spec[band:, :band] - spec[:band, band:]

    @pl.when(step == 0)
    def _():
        for k in range(kernels):
            weight = jnp.full((band, LANES), weights_ref[k], jnp.float32)
            scale = jnp.sqrt(weight) / (pad_side * band * GAIN_GRID**2)
            for part in range(2):
                load_kern(part, k).wait()
                kern_s[part, k] = kern_s[part, k] * scale

    for k in range(kernels):
        amp_re = low(kern_s[0, k] * spec_re - kern_s[1, k] * spec_im)
        amp_im = low(kern_s[0, k] * spec_im + kern_s[1, k] * spec_re)
        upper = jnp.concatenate([amp_re, amp_im], axis=1)
        lower = jnp.concatenate([-amp_im, amp_re], axis=1)
        half = low(dot(cs_g_t_ref[...], jnp.concatenate([upper, lower], axis=0)))
        half_s[:, k] = half.reshape(blocks, STRIP, grid)
    for b in range(0, blocks, GROUP):
        lines = half_s[b : b + GROUP].reshape(GROUP * kernels * STRIP, grid)
        field = dot(lines, field_ref[...])
        re = field[:, :grid]
        im = field[:, grid:]
        power = (re * re + im * im).reshape(GROUP, kernels, STRIP, grid)
        level_s[b : b + GROUP] = jnp.sum(power, axis=1)
        field_s[b : b + GROUP] = low(field).reshape(GROUP, kernels, STRIP, 2 * grid)
    level = level_s[...].reshape(grid, grid)
    mean = jnp.sum(jnp.sum(level, axis=0, keepdims=True), axis=1, keepdims=True) / (grid * grid)
    lines = low(dot(spread_ref[...], low(level - mean)))
    above = (mean - resist_level) * (0.5 * resist_gain)
    swing = jnp.tanh(dot(lines, spread_t_ref[...]) * (0.5 * resist_gain / GAIN_SPREAD**2) + above)
    resist = 0.5 * swing + 0.5
    resist_ref[...] = resist
    top = resist_gain / GAIN_SPREAD**2
    slopes = (resist - target_ref[...]) * (top - top * (swing * swing))
    lines = low(dot(spread_t_ref[...], low(slopes)))
    pulls = low(dot(lines, spread_ref[...])).reshape(blocks, 1, STRIP, grid)
    for b in range(0, blocks, GROUP):
        pull = jnp.concatenate([pulls[b : b + GROUP]] * 2, axis=3)
        back = field_s[b : b + GROUP] * pull
        bhalf = low(dot(back.reshape(GROUP * kernels * STRIP, 2 * grid), field_t_ref[...]))
        bhalf = bhalf.reshape(GROUP, kernels, STRIP, grid)
        for g in range(GROUP):
            bhalf_s[:, b + g] = bhalf[g]
    bspec_re = jnp.zeros((band, band), jnp.float32)
    bspec_im = jnp.zeros((band, band), jnp.float32)
    for k in range(kernels):
        bamp = dot(cs_g_ref[...], bhalf_s[k].reshape(grid, grid))
        bamp_re = bamp[:band, :band] + bamp[band:, band:]
        bamp_im = bamp[:band, band:] - bamp[band:, :band]
        bspec_re += kern_s[0, k] * bamp_re + kern_s[1, k] * bamp_im
        bspec_im += kern_s[0, k] * bamp_im - kern_s[1, k] * bamp_re
    upper = jnp.concatenate([low(bspec_re), low(-bspec_im)], axis=1)
    lower = jnp.concatenate([low(bspec_im), low(bspec_re)], axis=1)
    bforw = low(dot(jnp.concatenate([upper, lower], axis=0), cs_in_ref[...]))
    gradient = dot(cs_in_t_ref[...], bforw)
    shading = windows_s[here, HALO : HALO + tile, LANES : LANES + tile].astype(jnp.float32)
    grad_param = gradient * (1.0 - shading * shading)
    new_free_ref[...] = free_ref[...] - step_free * grad_param
    turned_s[0] = grad_param
    plain = low(grad_param)
    group = flip_ref.shape[0]
    for at in range(0, tile, group):
        part = slice(at, at + group)
        across = dot(plain[:, part], flip_ref[...])
        turned_s[2, :, part] = across
        for f, source in ((1, plain[:, part]), (3, low(across))):
            for up in range(0, tile, group):
                turned_s[f, up : up + group, part] = dot(flip_ref[...], source[up : up + group])
    cells = tile // CELL
    left = left_mask(CELL)

    def cells_step(a, carry):
        rows = pl.ds(pl.multiple_of(a * CELL, CELL), CELL)
        for pair in range(cells // 2):
            s0, s1, o0, o1 = pair_codes(
                inst_ref, orient_ref, owner_ref, i * cells + a, j * cells + 2 * pair
            )
            lanes = slice(pair * LANES, (pair + 1) * LANES)
            left_s[s0] += turned_s[o0, rows, lanes]
            right_s[s1] += turned_s[o1, rows, lanes]
        return carry

    lax.fori_loop(0, cells, cells_step, 0)

    @pl.when((i == pl.num_programs(0) - 1) & (j == pl.num_programs(1) - 1))
    def _():
        stored = sums_ref.shape[0] // n_col
        share = stored // n_row

        def pack(p, carry):
            one = left_s[2 * p] + pltpu.roll(right_s[2 * p], CELL, 1)
            two = pltpu.roll(left_s[2 * p + 1], CELL, 1) + right_s[2 * p + 1]
            col = p // stored
            row = p % stored // share
            side = row % 2 * (n_col // 2) + col // 2
            spot = (side * n_row + row // 2 * 2 + col % 2) * share + p % share
            sums_ref[spot] = low(jnp.where(left, one, two))
            return carry

        lax.fori_loop(0, sums_ref.shape[0], pack, 0, unroll=4)


def tile_steps(
    inst, orient, owner, weights, padded, target, free, spectra, consts, flip, masters, n_row, n_col
):
    height, width = target.shape
    band, kernels = spectra.shape[1:3]
    grid = 2 * band
    blocks = grid // STRIP
    tile_spec = pl.BlockSpec((TILE, TILE), lambda i, j, *_: (i, j))
    hbm = pl.BlockSpec(memory_space=pltpu.HBM)
    sums_shape = (masters // 2, CELL, LANES)
    return pl.pallas_call(
        functools.partial(tile_kernel, n_row, n_col),
        grid_spec=pltpu.PrefetchScalarGridSpec(
            num_scalar_prefetch=4,
            grid=(height // TILE, width // TILE),
            in_specs=[hbm, tile_spec, tile_spec, hbm, *[VM] * len(consts), VM],
            out_specs=[tile_spec, tile_spec, VM],
            scratch_shapes=[
                pltpu.VMEM((2, TILE + 2 * HALO, TILE + 2 * LANES), jnp.bfloat16),
                pltpu.VMEM((2, kernels, band, band), jnp.float32),
                pltpu.VMEM((blocks, kernels, STRIP, grid), jnp.bfloat16),
                pltpu.VMEM((blocks, kernels, STRIP, 2 * grid), jnp.bfloat16),
                pltpu.VMEM((kernels, blocks, STRIP, grid), jnp.bfloat16),
                pltpu.VMEM((blocks, STRIP, grid), jnp.float32),
                pltpu.VMEM((4, TILE, TILE), jnp.float32),
                pltpu.VMEM((masters, CELL, LANES), jnp.float32),
                pltpu.VMEM((masters, CELL, LANES), jnp.float32),
                pltpu.SemaphoreType.DMA((2,)),
                pltpu.SemaphoreType.DMA((2, kernels)),
            ],
        ),
        out_shape=[
            jax.ShapeDtypeStruct(target.shape, jnp.float32),
            jax.ShapeDtypeStruct(target.shape, jnp.float32),
            jax.ShapeDtypeStruct(sums_shape, jnp.bfloat16),
        ],
        compiler_params=pltpu.CompilerParams(vmem_limit_bytes=TILE_MIB * 1024 * 1024),
        name="tile_steps",
    )(inst, orient, owner, weights, padded, target, free, spectra, *consts, flip)


def greet(peers):
    barrier = pltpu.get_barrier_semaphore()
    for peer in peers:
        pl.semaphore_signal(barrier, inc=1, device_id=peer, device_id_type=MESH)
    pl.semaphore_wait(barrier, len(peers))


def level_peers(n_row, n_col):
    r = lax.axis_index("row")
    c = lax.axis_index("col")
    long = n_col // 2
    z, y = lax.div(c, 2), lax.rem(c, 2)
    x, core = lax.div(r, 2), lax.rem(r, 2)
    p = x * 2 + y

    def z_at(t):
        return lax.rem(z + t + long, long)

    def p_at(t):
        q = lax.rem(p + t + n_row, n_row)
        return lax.div(q, 2), lax.rem(q, 2)

    return r, c, z, y, x, core, long, z_at, p_at


def gather_ids(n_row, n_col):
    r, c, z, y, x, core, long, z_at, p_at = level_peers(n_row, n_col)
    ids = [(r, z_at(t) * 2 + y) for t in range(1, long)]
    for t in range(1, n_row):
        px, py = p_at(t)
        ids.append((px * 2 + core, z * 2 + py))
    return ids + [(x * 2 + 1 - core, c)]


def gather_levels(n_row, n_col, own, table_ref, stored, send_sem, recv_sem, started, ready):
    r, c, z, y, x, core, long, z_at, p_at = level_peers(n_row, n_col)
    share = stored // n_row
    partner = (x * 2 + 1 - core, c)

    def first_row(row, col):
        return col * stored + row * share

    def make(src, at, level, slot, peer):
        return pltpu.make_async_remote_copy(
            src_ref=src,
            dst_ref=table_ref.at[pl.ds(at, share)],
            send_sem=send_sem.at[level, slot],
            recv_sem=recv_sem.at[level, slot],
            device_id=peer,
            device_id_type=MESH,
        )

    def here(at):
        return table_ref.at[pl.ds(at, share)]

    mine = first_row(r, c)
    first = [make(own, mine, 0, t, (r, z_at(t) * 2 + y)) for t in range(1, long)]
    for copy in first:
        copy.start()
    started()
    second = []
    third = []
    for t in range(long):
        if t > 0:
            first[t - 1].wait_recv()
        at = first_row(r, z_at(-t) * 2 + y)
        src = own if t == 0 else here(at)
        for q in range(1, n_row):
            px, py = p_at(q)
            copy = make(src, at, 1, t * n_row + q, (px * 2 + core, z * 2 + py))
            copy.start()
            second.append(copy)
        copy = make(src, at, 2, t * n_row, partner)
        copy.start()
        third.append(copy)
    ready([first_row(r, z_at(-t) * 2 + y) for t in range(long)])

    def across(n):
        t = n // (n_row - 1)
        q = n % (n_row - 1) + 1
        px, py = p_at(-q)
        at = first_row(px * 2 + core, z_at(-t) * 2 + py)
        slot = t * n_row + q
        make(here(at), at, 1, slot, partner).wait_recv()
        make(here(at), at, 2, slot, partner).start()
        return at

    def beside(t, q):
        px, py = p_at(-q)
        at = first_row(px * 2 + 1 - core, z_at(-t) * 2 + py)
        make(here(at), at, 2, t * n_row + q, partner).wait_recv()
        return at

    def later(n):
        return beside(n // (n_row - 1), n % (n_row - 1) + 1)

    def early(n, carry):
        ready([across(n), beside(n, 0)])
        return carry

    def middle(n, carry):
        ready([across(n), later(n - long)])
        return carry

    def late(n, carry):
        ready([later(2 * n), later(2 * n + 1)])
        return carry

    count = long * (n_row - 1)
    lax.fori_loop(0, long, early, 0)
    lax.fori_loop(long, count, middle, 0)
    lax.fori_loop((count - long) // 2, count // 2, late, 0)

    def sent(n, carry):
        make(here(mine), mine, 2, n, partner).wait_send()
        return carry

    for copy in first + second:
        copy.wait_send()
    lax.fori_loop(0, long * n_row, sent, 0)


def gather_sems(n_row, n_col):
    shape = (3, n_row * n_col // 2)
    return [pltpu.SemaphoreType.DMA(shape), pltpu.SemaphoreType.DMA(shape)]


def pack_rows(rows_ref, lines_s, out_ref):
    left = left_mask(HALF)
    for pair in range(out_ref.shape[0]):
        halves = []
        for e in range(2):
            for n in range(HALF):
                at = 2 * pair + e
                lines_s[at, n : n + 1] = rows_ref[at : at + 1, n * LANES : (n + 1) * LANES]
            halves.append(lines_s[2 * pair + e])
        one, two = halves
        even = jnp.where(left, one, pltpu.roll(two, CELL, 1))
        odd = jnp.where(left, pltpu.roll(one, CELL, 1), two)
        out_ref[pair, pl.ds(0, HALF, stride=2)] = even
        out_ref[pair, pl.ds(1, HALF, stride=2)] = odd


def front_kernel(
    n_row, n_col, codes_refs, rows_hbm, free_ref, flip_hbm, spread_hbm, out_hbm, own_ref,
    out_ref, codes_s, rows_s, lines_s, cells_s, share_s, table_s, turned_s, free_s, flip_ref, spread_ref,
    edge_l, edge_r, from_l, from_r,
    load_sem, save_sem, send_sem, recv_sem, halo_send, halo_recv,
):
    r = lax.axis_index("row")
    c = lax.axis_index("col")
    height, width = free_s.shape
    packed = height // 2
    stored = rows_s.shape[0] // 2
    share = stored // n_row
    inst_ref, orient_ref, owner_ref = codes_s
    loads = [(rows_hbm, rows_s), (flip_hbm, flip_ref), (spread_hbm, spread_ref)]
    loads += [*zip(codes_refs, codes_s), (free_ref, free_s)]
    loads = [pltpu.make_async_copy(src, dst, load_sem.at[n]) for n, (src, dst) in enumerate(loads)]
    for load in loads:
        load.start()
    loads[0].wait()
    pack_rows(rows_s, lines_s, cells_s)
    own_ref[...] = cells_s[pl.ds(r * share, share)]
    share_s[...] = own_ref[...].astype(jnp.bfloat16)
    moves = [(0, 1), (0, -1), (1, 0), (-1, 0), (1, 1), (1, -1), (-1, 1), (-1, -1)]
    ids = [(lax.rem(r + n_row + dr, n_row), lax.rem(c + n_col + dc, n_col)) for dr, dc in moves]
    greet(gather_ids(n_row, n_col) + ids)
    table_s[pl.ds(c * stored + r * share, share)] = share_s[...]

    def started():
        loads[1].wait()
        loads[2].wait()

    def save(n, *at):
        return pltpu.make_async_copy(out_ref.at[at], out_hbm.at[at], save_sem.at[n])

    def ready(spots):
        turn_blocks(table_s, turned_s, flip_ref, spread_ref, spots, share)

    gather_levels(n_row, n_col, share_s, table_s, stored, send_sem, recv_sem, started, ready)
    for load in loads[3:]:
        load.wait()

    pairs = width // LANES
    strips = height // CELL
    cast = lambda v: v.astype(jnp.bfloat16)
    left = left_mask(HALF)

    def draw(a, pair):
        codes = pair_codes(inst_ref, orient_ref, owner_ref, a, 2 * pair)
        cells = assemble_pair(turned_s, codes)
        rows = pl.ds(pl.multiple_of(a * CELL, CELL), CELL)
        value = jnp.tanh(cells + free_s[rows, pair * LANES : (pair + 1) * LANES])
        rows = pl.ds(pl.multiple_of(HALO + a * CELL, CELL), CELL)
        out_ref[rows, (pair + 1) * LANES : (pair + 2) * LANES] = cast(value)
        return value

    def outer(n, carry):
        for pair in range(1, pairs - 1):
            draw(n * (strips - 1), pair)
        return carry

    def sides(a, carry):
        rows = pl.ds(pl.multiple_of(a * HALF, HALF), HALF)
        value = draw(a, 0)
        edge_l[rows] = cast(jnp.where(left, value[:HALF], pltpu.roll(value[HALF:], CELL, 1)))
        value = draw(a, pairs - 1)
        edge_r[rows] = cast(jnp.where(left, pltpu.roll(value[:HALF], CELL, 1), value[HALF:]))
        return carry

    def inner(a, carry):
        for pair in range(1, pairs - 1):
            draw(a, pair)
        return carry

    lax.fori_loop(0, 2, outer, 0)
    lax.fori_loop(0, strips, sides, 0)
    lax.fori_loop(1, 3, inner, 0)

    middle = slice(LANES, LANES + width)
    row_parts = {
        -1: (slice(HALO, 2 * HALO), slice(HALO + height, 2 * HALO + height)),
        1: (slice(height, HALO + height), slice(0, HALO)),
    }
    edge_parts = {
        -1: (slice(0, HALF), slice(HALF + packed, 2 * HALF + packed)),
        0: (slice(0, packed), slice(HALF, HALF + packed)),
        1: (slice(packed - HALF, packed), slice(0, HALF)),
    }

    def inside(dr, dc):
        return (r + dr >= 0) & (r + dr < n_row) & (c + dc >= 0) & (c + dc < n_col)

    work = []
    for at, (dr, dc) in enumerate(moves):
        if dc == 0:
            src, dst = row_parts[dr]
            src, dst = out_ref.at[src, middle], out_ref.at[dst, middle]
        else:
            src, dst = edge_parts[dr]
            src = (edge_r if dc == 1 else edge_l).at[src]
            dst = (from_l if dc == 1 else from_r).at[dst]
        copy = pltpu.make_async_remote_copy(
            src_ref=src,
            dst_ref=dst,
            send_sem=halo_send.at[at],
            recv_sem=halo_recv.at[at],
            device_id=ids[at],
            device_id_type=MESH,
        )
        work.append((copy, dst, inside(dr, dc), inside(-dr, -dc)))
    for copy, dst, sends, gets in work:
        pl.when(sends)(copy.start)
    lax.fori_loop(3, strips - 1, inner, 0)
    lines = slice(HALO, HALO + height)
    saves = [save(0, lines, middle)]
    for copy in saves:
        copy.start()
    for copy, dst, sends, gets in work:

        @pl.when(jnp.logical_not(gets))
        def _():
            dst[...] = jnp.zeros(dst.shape, dst.dtype)

    for copy, dst, sends, gets in work:
        pl.when(gets)(copy.wait_recv)

    def unpack(a, carry):
        rows = pl.ds(pl.multiple_of(a * HALF, HALF), HALF)
        upper = pl.ds(pl.multiple_of(a * CELL, CELL), HALF)
        lower = pl.ds(pl.multiple_of(a * CELL + HALF, HALF), HALF)
        one = from_l[rows].astype(jnp.float32)
        two = from_r[rows].astype(jnp.float32)
        last = slice(LANES + width, 2 * LANES + width)
        out_ref[upper, :LANES] = cast(jnp.where(left, 0.0, pltpu.roll(one, CELL, 1)))
        out_ref[lower, :LANES] = cast(jnp.where(left, 0.0, one))
        out_ref[upper, last] = cast(jnp.where(left, two, 0.0))
        out_ref[lower, last] = cast(jnp.where(left, pltpu.roll(two, CELL, 1), 0.0))
        return carry

    lax.fori_loop(0, (height + 2 * HALO) // CELL, unpack, 0)
    last = [
        save(1, slice(0, HALO)),
        save(2, slice(HALO + height, 2 * HALO + height)),
        save(3, lines, slice(0, LANES)),
        save(4, lines, slice(LANES + width, 2 * LANES + width)),
    ]
    for copy in last:
        copy.start()
    for copy, dst, sends, gets in work:
        pl.when(sends)(copy.wait_send)
    for copy in saves + last:
        copy.wait()


def front(codes, masters, free, flip, spread, n_row, n_col):
    height, width = free.shape
    hbm = pl.BlockSpec(memory_space=pltpu.HBM)
    low = jnp.bfloat16
    stored = masters.shape[0] // 2
    pairs = n_col * stored
    cells = (CELL, LANES)
    edge = pltpu.VMEM((height // 2, LANES), low)
    edge_in = pltpu.VMEM((height // 2 + 2 * HALF, LANES), low)
    return pl.pallas_call(
        functools.partial(front_kernel, n_row, n_col),
        in_specs=[[hbm] * 3, hbm, hbm, hbm, hbm],
        out_specs=[hbm, VM],
        out_shape=[
            jax.ShapeDtypeStruct((height + 2 * HALO, width + 2 * LANES), low),
            jax.ShapeDtypeStruct((stored // n_row,) + cells, jnp.float32),
        ],
        scratch_shapes=[
            pltpu.VMEM((height + 2 * HALO, width + 2 * LANES), low),
            [pltpu.SMEM(v.shape, v.dtype) for v in codes],
            pltpu.VMEM(masters.shape, jnp.float32),
            pltpu.VMEM((2 * stored, HALF, LANES), jnp.float32),
            pltpu.VMEM((stored,) + cells, jnp.float32),
            pltpu.VMEM((stored // n_row,) + cells, low),
            pltpu.VMEM((pairs,) + cells, low),
            pltpu.VMEM((8 * pairs,) + cells, low),
            pltpu.VMEM((height, width), jnp.float32),
            pltpu.VMEM(flip.shape, low),
            pltpu.VMEM(spread.shape, low),
            edge, edge, edge_in, edge_in,
            pltpu.SemaphoreType.DMA((7,)),
            pltpu.SemaphoreType.DMA((5,)),
            *gather_sems(n_row, n_col),
            pltpu.SemaphoreType.DMA((8,)),
            pltpu.SemaphoreType.DMA((8,)),
        ],
        compiler_params=pltpu.CompilerParams(
            collective_id=0, has_side_effects=True, vmem_limit_bytes=FRONT_MIB * 1024 * 1024
        ),
        name="front",
    )(codes, masters, free, flip, spread)


def smooth_packed(cells):
    count = cells.shape[0]
    flat = cells.reshape(count * CELL, LANES)
    x = lax.broadcasted_iota(jnp.int32, flat.shape, 1) % CELL
    y = lax.broadcasted_iota(jnp.int32, flat.shape, 0) % CELL
    before = jnp.where(x == 0, 0.0, pltpu.roll(flat, 1, 1))
    after = jnp.where(x == CELL - 1, 0.0, pltpu.roll(flat, LANES - 1, 1))
    up = jnp.where(y == 0, 0.0, pltpu.roll(flat, 1, 0))
    down = jnp.where(y == CELL - 1, 0.0, pltpu.roll(flat, count * CELL - 1, 0))
    return (0.5 * flat + 0.125 * (before + after + up + down)).reshape(cells.shape)


def update_kernel(
    n_row, n_col, sums_ref, own_ref, flip_ref, spread_ref, turned_ref, fresh_ref,
    table_s, fresh, rc, mid, rp, zb, rz,
    core_send, core_recv, p_send, p_recv, z_send, z_recv, send_sem, recv_sem,
):
    r, c, z, y, x, core, long, z_at, p_at = level_peers(n_row, n_col)
    p = x * 2 + y
    share = own_ref.shape[0]
    stored = share * n_row
    low = lambda v: v.astype(jnp.bfloat16)
    high = lambda v: v.astype(jnp.float32)
    greet(gather_ids(n_row, n_col))
    order = [*range(1, long), 0]

    def make(src, dst, send, recv, at, peer):
        return pltpu.make_async_remote_copy(
            src_ref=src,
            dst_ref=dst,
            send_sem=send.at[at],
            recv_sem=recv.at[at],
            device_id=peer,
            device_id_type=MESH,
        )

    def chunk(side, t):
        return pl.ds((side * long + z_at(t)) * stored, stored)

    to_core = {}
    for t in order:
        src = sums_ref.at[chunk(1 - core, t)]
        to_core[t] = make(src, rc.at[t], core_send, core_recv, t, (x * 2 + 1 - core, c))
        to_core[t].start()
    to_p = {}
    for t in order:
        to_core[t].wait_recv()
        mid[t] = low(high(sums_ref[chunk(core, t)]) + high(rc[t]))
        for q in range(1, n_row):
            px, py = p_at(q)
            src = mid.at[t, pl.ds((px * 2 + py) * share, share)]
            at = t * n_row + q
            to_p[at] = make(src, rp.at[at], p_send, p_recv, at, (px * 2 + core, z * 2 + py))
            to_p[at].start()
    to_z = {}
    for t in order:
        total = high(mid[t, pl.ds(p * share, share)])
        for q in range(1, n_row):
            at = t * n_row + q
            to_p[at].wait_recv()
            total = total + high(rp[at])
        if t > 0:
            zb[t] = low(total)
            to_z[t] = make(zb.at[t], rz.at[t], z_send, z_recv, t, (r, z_at(t) * 2 + y))
            to_z[t].start()
    for t in range(1, long):
        to_z[t].wait_recv()
        total = total + high(rz[t])
    updated = own_ref[...] - step_master * total
    value = low(smooth_packed(updated))
    fresh[...] = value
    table_s[pl.ds(c * stored + r * share, share)] = value

    def ready(spots):
        turn_blocks(table_s, turned_ref, flip_ref, spread_ref, spots, share)

    gather_levels(n_row, n_col, fresh, table_s, stored, send_sem, recv_sem, lambda: None, ready)
    fresh_ref[...] = high(table_s[pl.ds(c * stored, stored)])
    for copy in [*to_core.values(), *to_p.values(), *to_z.values()]:
        copy.wait_send()


def update_masters(sums, own, flip, spread, n_row, n_col):
    share = own.shape[0]
    stored = share * n_row
    long = n_col // 2
    low = jnp.bfloat16
    cells = (CELL, LANES)
    sems = [pltpu.SemaphoreType.DMA((n,)) for n in (long, long, long * n_row, long * n_row, long, long)]
    return pl.pallas_call(
        functools.partial(update_kernel, n_row, n_col),
        in_specs=[VM, VM, VM, VM],
        out_specs=[VM, VM],
        out_shape=[
            jax.ShapeDtypeStruct((8 * sums.shape[0],) + cells, low),
            jax.ShapeDtypeStruct((stored,) + cells, jnp.float32),
        ],
        scratch_shapes=[
            pltpu.VMEM(sums.shape, low),
            pltpu.VMEM((share,) + cells, low),
            pltpu.VMEM((long, stored) + cells, low),
            pltpu.VMEM((long, stored) + cells, low),
            pltpu.VMEM((long * n_row, share) + cells, low),
            pltpu.VMEM((long, share) + cells, low),
            pltpu.VMEM((long, share) + cells, low),
            *sems,
            *gather_sems(n_row, n_col),
        ],
        compiler_params=pltpu.CompilerParams(
            collective_id=2, has_side_effects=True, vmem_limit_bytes=UPDATE_MIB * 1024 * 1024
        ),
        name="update_masters",
    )(sums, own, flip, spread)


def per_device(
    masters, inst_master, inst_orient, owner_map, tile_free, target, kernel_spectra, socs_weights
):
    stored = masters.shape[0] // 2
    total = owner_map.shape[0]
    consts = tables(TILE + 2 * HALO, kernel_spectra.shape[1], HALO, TILE)
    flip, spread = flips()
    n_row = lax.axis_size("row")
    n_col = lax.axis_size("col")
    codes = [inst_master, inst_orient, owner_map]
    padded, own = front(codes, masters, tile_free, flip, spread, n_row, n_col)
    resist, new_free, sums = tile_steps(
        *codes, socs_weights, padded, target, tile_free, kernel_spectra, consts, flip, total,
        n_row, n_col,
    )
    turned, fresh = update_masters(sums, own, flip, spread, n_row, n_col)
    new_mask = image(inst_master, inst_orient, owner_map, turned, new_free)
    fresh = fresh.reshape(stored, CELL, 2, CELL).transpose(0, 2, 1, 3)
    return (resist, new_mask, fresh.reshape(masters.shape))


def solution(mesh):
    in_specs = (
        P("col", None),
        P("row", "col"),
        P("row", "col"),
        P(),
        P("row", "col"),
        P("row", "col"),
        P(),
        P(),
    )
    out_specs = (P("row", "col"), P("row", "col"), P("col", None))
    return jax.shard_map(
        per_device, mesh=mesh, in_specs=in_specs, out_specs=out_specs, check_vma=False
    )
```
